512 devices in a mesh: seq: 16 (over z, core), head: 32 (over x, y).
Axes of the slice: x: 4, y: 8, z: 8, core: 2. Of those that a mesh axis runs over, the one named last changes fastest.
Arguments:
- x_in: bfloat16 [16384, 16384], P('seq', 'head'), may hold values from -40 to 40
- z_gate: bfloat16 [16384, 16384], P('seq', 'head'), may hold values from -6 to 6
- b_input: bfloat16 [16384, 8, 128], P('seq'), may hold values from -2 to 2
- c_input: bfloat16 [16384, 8, 128], P('seq'), may hold values from -2 to 2
- dt_raw: float32 [128, 16384], P('head', 'seq'), may hold values from -5 to 5462
- a_log: float32 [128], P('head'), may hold values from -20 to 0
- d_skip: float32 [128], P('head'), may hold values from 0.5 to 2
- norm_gain: float32 [16384], P('head'), may hold values from 0.25 to 1.75
- doc_lengths: int32 [6], replicated, may hold values from 1 to 5461, 16384 in all
- doc_lang: int32 [6], replicated, may hold values from 0 to 3
- adapt_down: bfloat16 [4, 16384, 128], P(None, 'head'), may hold values from -0.046875 to 0.046875
- adapt_up: bfloat16 [4, 128, 16384], P(None, None, 'head'), may hold values from -0.5 to 0.5
Outputs:
- adapted: bfloat16 [16384, 16384], P('seq', 'head')
The draws below stay inside these ranges and needn't reach their ends.
Inputs may be any that keep to these rules, and one draw needn't show every extreme that they name: `doc_lengths`: the lengths sum to 16384; the longest document has exactly 5461 tokens.
All inputs are finite; a program needn't handle non-finite values.
Results may differ from the reference program's by a relative error of at most 0.0075.
Values may be sent and summed in bfloat16 or wider, within the bound.
A program may use at most 64 MiB of HBM per device.

```python
import math
import jax
import jax.numpy as jnp
import numpy as np
from jax import lax

SPACE_HEADS = 128
HEAD_DIM = 128
STATE = 128
GROUPS = 8
RANK = 128
NLANG = 4
NDOC = 6
STREAM_TOKENS = 16384
D_INNER = 16384
MOST_LEN = 5461


def decay_layout(key):
    base_key = jax.random.fold_in(key, 7)
    key_kind, key_fast, key_slow, random_key_locations, random_key_penalty, random_key_jitter = jax.random.split(base_key, 6)
    slow_share = 0.5
    slow_heads = jax.random.uniform(key_kind, (SPACE_HEADS,)) < slow_share
    fast_span = jnp.exp(jax.random.uniform(key_fast, (SPACE_HEADS,), minval=jnp.log(30.0), maxval=jnp.log(50.0)))
    fast_rate = 1.0 / (0.2 * fast_span)
    slow_rate = jnp.exp(jax.random.uniform(key_slow, (SPACE_HEADS,), minval=jnp.log(0.3), maxval=jnp.log(0.8))) / (0.2 * STREAM_TOKENS)
    spike_amplitude = jnp.where(slow_heads, slow_rate, fast_rate)
    spike_locations = jax.random.randint(random_key_locations, (2,), 0, STREAM_TOKENS)
    spike_penalty = jax.random.uniform(random_key_penalty, (SPACE_HEADS, 2), minval=0.22, maxval=0.5)
    return (spike_amplitude, spike_locations, spike_penalty, random_key_jitter)


def dt_table(key):
    spike_amplitude, spike_locations, spike_penalty, random_key_jitter = decay_layout(key)
    noise = jnp.clip(jax.random.normal(random_key_jitter, (SPACE_HEADS, STREAM_TOKENS), jnp.float32), -2.5, 2.5)
    starting_values = -2.0 + noise
    token_positions = jnp.arange(STREAM_TOKENS)
    match_count = token_positions[None, :, None] == spike_locations[None, None, :]
    expected_output = jnp.sum(jnp.where(match_count, (spike_penalty / spike_amplitude[:, None])[:, None, :], 0.0), axis=2)
    spike_flags = jnp.any(match_count, axis=2)
    return jnp.where(spike_flags, expected_output, starting_values)


def draw_dt_raw(key, part):
    return dt_table(key).astype(jnp.float32)


def draw_a_log(key, part):
    spike_amplitude, spike_locations, spike_penalty, random_key_jitter = decay_layout(key)
    return jnp.log(spike_amplitude).astype(jnp.float32)


def draw_x_in(key, part):
    step_dt = jax.nn.softplus(dt_table(key))
    key_values = jax.random.fold_in(key, 19)
    values = jnp.clip(jax.random.normal(key_values, (STREAM_TOKENS, SPACE_HEADS, HEAD_DIM), jnp.float32), -4.0, 4.0)
    rising = 3.0 ** (jnp.arange(SPACE_HEADS, dtype=jnp.float32) / max(SPACE_HEADS - 1, 1))
    scaling = rising[None, :] * jnp.minimum(1.0, 1.0 / step_dt).T
    return (values * scaling[:, :, None]).reshape(STREAM_TOKENS, D_INNER).astype(jnp.bfloat16)


def plant(array, own_key, low, largest):
    extent = array.shape
    spot = [jax.random.randint(jax.random.fold_in(own_key, axis), (), 0, extent[axis]) for axis in range(len(extent))]
    array = array.at[tuple(spot)].set(low)
    longest = extent.index(max(extent))
    spot[longest] = (spot[longest] + 1) % extent[longest]
    return array.at[tuple(spot)].set(largest)


def block_scale(stream_key, dims, shards, low, high):
    def one(position, parts):
        heights = jax.random.uniform(jax.random.fold_in(jax.random.fold_in(stream_key, 6), position), (parts,), jnp.float32, low / len(shards), high / len(shards))
        return jnp.repeat(jnp.exp(heights), dims[position] // parts).reshape((-1,) + (1,) * (len(dims) - position - 1))

    loudness = one(*shards[0])
    for cut in shards[1:]:
        loudness = loudness * one(*cut)
    return loudness


def length_profile(amount, total, most, lean):
    portions = [(1 << 20) // math.isqrt(standing ** lean) + 1 for standing in range(2, amount + 1)]
    surplus, given = total - most - (amount - 1), [1] * (amount - 1)
    while surplus > 0:
        candidates = [i for i in range(amount - 1) if given[i] < most]
        whole, remaining = sum([portions[i] for i in candidates]), surplus
        for i in candidates:
            more = min(most - given[i], max(1, remaining * portions[i] // whole), surplus)
            given[i] = given[i] + more
            surplus = surplus - more
    return np.array([most] + given)


def uneven(own_key, amount, total, limit, slope):
    if amount == 2:
        one = jax.random.randint(own_key, (), max(1, total - limit), min(limit, total - 1) + 1)
        return jnp.stack([one, total - one])
    lengths = jnp.asarray(length_profile(amount, total, limit, slope), jnp.int32)
    twos = (amount - 1) // 2
    source_of, sink = lengths[1:1 + 2 * twos:2], lengths[2:2 + 2 * twos:2]
    slack = jnp.minimum(source_of - 1, limit - sink)
    passed = jax.random.randint(jax.random.fold_in(own_key, 1), (twos,), 0, 1 << 20) % (slack + 1)
    lengths = lengths.at[1:1 + 2 * twos:2].set(source_of - passed).at[2:2 + 2 * twos:2].set(sink + passed)
    return lengths[jax.random.permutation(jax.random.fold_in(own_key, 2), amount)]


def centred(rng, dims, width, reach, cuts=(), kind=jnp.bfloat16):
    drawn = jax.random.normal(rng, dims, jnp.float32) * width
    if len(cuts) > 0:
        drawn = block_scale(rng, dims, cuts, -0.22, 0.18) * drawn
    return jnp.clip(drawn, min=-reach, max=reach).astype(kind)


def setup_inputs(seed: int = 0) -> dict:
    arg_keys = jax.random.split(jax.random.key(seed), 13)
    x_in = draw_x_in(jax.random.fold_in(arg_keys[12], 71), 0)
    z_gate = centred(arg_keys[1], (STREAM_TOKENS, D_INNER), 1.0, 6.0, ((0, 16), (1, 32)))
    b_input = centred(arg_keys[2], (STREAM_TOKENS, GROUPS, STATE), 0.3, 2.0, ((0, 16),))
    c_input = centred(arg_keys[3], (STREAM_TOKENS, GROUPS, STATE), 0.3, 2.0, ((0, 16),))
    dt_raw = draw_dt_raw(jax.random.fold_in(arg_keys[12], 71), 0)
    a_log = draw_a_log(jax.random.fold_in(arg_keys[12], 71), 0)
    d_skip = jnp.clip(0.5 + 1.5 * jax.random.uniform(arg_keys[6], (SPACE_HEADS,), jnp.float32) ** block_scale(arg_keys[6], (SPACE_HEADS,), ((0, 32),), -0.2, 0.2), 0.5, 2.0)
    norm_gain = jnp.clip(1.0 + 0.15 * jax.random.normal(arg_keys[7], (D_INNER,), jnp.float32), 0.25, 1.75)
    doc_lengths = uneven(arg_keys[8], NDOC, STREAM_TOKENS, MOST_LEN, 2).astype(jnp.int32)
    doc_lang = plant(jax.random.randint(arg_keys[9], (NDOC,), 0, NLANG), jax.random.fold_in(arg_keys[9], 1), 0, NLANG - 1).astype(jnp.int32)
    adapt_down = centred(arg_keys[10], (NLANG, D_INNER, RANK), D_INNER ** -0.5, 0.046875, ((1, 32),))
    adapt_up = centred(arg_keys[11], (NLANG, RANK, D_INNER), RANK ** -0.5, 0.5, ((2, 32),))
    return dict(x_in=x_in, z_gate=z_gate, b_input=b_input, c_input=c_input, dt_raw=dt_raw, a_log=a_log, d_skip=d_skip, norm_gain=norm_gain, doc_lengths=doc_lengths, doc_lang=doc_lang, adapt_down=adapt_down, adapt_up=adapt_up)


highest = lax.Precision.HIGHEST

def doc_tables(doc_lengths, doc_lang, token_positions, lang_count):
    doc_ends = jnp.cumsum(doc_lengths).astype(jnp.int32)
    doc_start = (doc_ends - doc_lengths).astype(jnp.int32)
    doc_index = lax.optimization_barrier(jnp.sum((token_positions[:, None] >= doc_start[None, :]).astype(jnp.int32), axis=1)).astype(jnp.int32) - 1
    is_first = lax.optimization_barrier(jnp.sum((token_positions[:, None] == doc_start[None, :]).astype(jnp.int32), axis=1)).astype(jnp.int32)
    doc_hot = (doc_index[:, None] == jnp.arange(doc_lengths.shape[0], dtype=jnp.int32)[None, :]).astype(jnp.int32)
    lang_index = lax.optimization_barrier(jnp.sum(doc_hot * doc_lang[None, :], axis=1)).astype(jnp.int32)
    lang_hot = lang_index[:, None] == jnp.arange(lang_count, dtype=jnp.int32)[None, :]
    return (doc_index, is_first, lang_hot)

def block_scan(x_vals, step_dt, log_decay, b_vals, c_vals, doc_index, is_first):
    head_count, length, head_width = x_vals.shape
    states = b_vals.shape[1]
    block_len = min(128, length)
    block_count = length // block_len
    x_blocks = x_vals.reshape(head_count, block_count, block_len, head_width).transpose(1, 0, 2, 3)
    dt_blocks = step_dt.reshape(head_count, block_count, block_len).transpose(1, 0, 2)
    dec_blocks = log_decay.reshape(head_count, block_count, block_len).transpose(1, 0, 2)
    b_blocks = b_vals.reshape(block_count, block_len, states)
    c_blocks = c_vals.reshape(block_count, block_len, states)
    doc_blocks = doc_index.reshape(block_count, block_len)
    first_blocks = is_first.reshape(block_count, block_len)
    lower_mask = jnp.arange(block_len)[:, None] >= jnp.arange(block_len)[None, :]

    def advance(carry_state, pieces):
        x_block, dt_block, dec_block, b_block, c_block, doc_block, first_block = pieces
        cumulative = jnp.cumsum(dec_block, axis=1)
        keep_mask = lower_mask & (doc_block[:, None] == doc_block[None, :])
        decay_gaps = jnp.where(keep_mask[None], cumulative[:, :, None] - cumulative[:, None, :], 0.0)
        scores = jnp.dot(c_block, b_block.T, preferred_element_type=jnp.float32)
        weights = jnp.where(keep_mask[None], jnp.exp(decay_gaps), 0.0) * scores[None] * dt_block[:, None, :]
        x_float = x_block.astype(jnp.float32)
        inner_part = jnp.einsum('hij,hjp->hip', weights, x_float, precision=highest)
        reach_mask = (jnp.cumsum(first_block) == 0).astype(jnp.float32)
        carried = jnp.einsum('in,hnp->hip', c_block.astype(jnp.float32), carry_state, precision=highest)
        carried = carried * (jnp.exp(cumulative) * reach_mask[None])[:, :, None]
        tail_keep = doc_block == doc_block[-1]
        tail_gaps = jnp.where(tail_keep[None], cumulative[:, -1:] - cumulative, 0.0)
        fresh_weight = jnp.where(tail_keep[None], jnp.exp(tail_gaps), 0.0) * dt_block
        written = jnp.einsum('jn,hjp->hnp', b_block.astype(jnp.float32), x_float * fresh_weight[:, :, None], precision=highest)
        kept_share = jnp.exp(cumulative[:, -1]) * reach_mask[-1]
        return (carry_state * kept_share[:, None, None] + written, inner_part + carried)
    initial = jnp.zeros((head_count, states, head_width), jnp.float32)
    final_state, outputs = lax.scan(advance, initial, (x_blocks, dt_blocks, dec_blocks, b_blocks, c_blocks, doc_blocks, first_blocks))
    outputs = outputs.transpose(1, 0, 2, 3).reshape(head_count, length, head_width)
    return (outputs, final_state)

def reference(x_in, z_gate, b_input, c_input, dt_raw, a_log, d_skip, norm_gain, doc_lengths, doc_lang, adapt_down, adapt_up):
    token_positions = jnp.arange(STREAM_TOKENS, dtype=jnp.int32)
    doc_index, is_first, lang_hot = doc_tables(doc_lengths, doc_lang, token_positions, NLANG)
    step_dt = jax.nn.softplus(dt_raw)
    log_decay = step_dt * (-jnp.exp(a_log))[:, None]
    per_group = SPACE_HEADS // GROUPS
    x_heads = x_in.reshape(STREAM_TOKENS, GROUPS, per_group, HEAD_DIM).transpose(1, 2, 0, 3)
    dt_groups = step_dt.reshape(GROUPS, per_group, STREAM_TOKENS)
    dec_groups = log_decay.reshape(GROUPS, per_group, STREAM_TOKENS)
    b_groups = b_input.transpose(1, 0, 2)
    c_groups = c_input.transpose(1, 0, 2)

    def one_group(pieces):
        x_group, dt_group, dec_group, b_group, c_group = pieces
        outputs, final_state = block_scan(x_group, dt_group, dec_group, b_group, c_group, doc_index, is_first)
        return outputs
    ssd_heads = lax.map(one_group, (x_heads, dt_groups, dec_groups, b_groups, c_groups))
    ssd_rows = ssd_heads.transpose(2, 0, 1, 3).reshape(STREAM_TOKENS, D_INNER)
    skip_rows = jnp.repeat(d_skip, HEAD_DIM)
    ssd_rows = ssd_rows + skip_rows[None, :] * x_in.astype(jnp.float32)
    gated = ssd_rows * jax.nn.silu(z_gate.astype(jnp.float32))
    mean_square = lax.optimization_barrier(jnp.sum(gated * gated, axis=1)) / D_INNER
    normed = (gated * lax.rsqrt(mean_square + 1e-05)[:, None] * norm_gain[None, :]).astype(jnp.bfloat16)
    low_sum = jnp.zeros((STREAM_TOKENS, RANK), jnp.float32)
    for language in range(NLANG):
        product = jnp.dot(normed, adapt_down[language], preferred_element_type=jnp.float32)
        low_sum = low_sum + jnp.where(lang_hot[:, language:language + 1], product, 0.0)
    low_rank = low_sum.astype(jnp.bfloat16)
    selected = jnp.where(lang_hot[:, :, None], low_rank[:, None, :], jnp.zeros((), jnp.bfloat16)).reshape(STREAM_TOKENS, NLANG * RANK)
    lifted = jnp.dot(selected, adapt_up.reshape(NLANG * RANK, D_INNER), preferred_element_type=jnp.float32)
    return (normed.astype(jnp.float32) + lifted).astype(jnp.bfloat16)
```

```python
import functools

import jax
import jax.numpy as jnp
from jax import lax
from jax.experimental import pallas as pl
from jax.experimental.pallas import tpu as pltpu
from jax.sharding import PartitionSpec as P

SPACE_HEADS = 128
HEAD_DIM = 128
GROUPS = 8
L = 128
MESH = pl.DeviceIdType.MESH
F32 = jnp.float32
BF16 = jnp.bfloat16
HIGHEST = lax.Precision.HIGHEST


def nt(a, b, precision=None):
    return lax.dot_general(
        a, b, (((1,), (1,)), ((), ())), preferred_element_type=F32, precision=precision
    )


def mm(a, b, precision=None):
    return jnp.dot(a, b, preferred_element_type=F32, precision=precision)


def kernel_body(
    seq_n,
    xn,
    yn,
    doc_len,
    doc_lang,
    a_log,
    d_skip,
    dt_ref,
    gain_ref,
    x_hbm,
    z_hbm,
    b_hbm,
    c_hbm,
    down_hbm,
    up_hbm,
    out_hbm,
    x_s,
    z_s,
    b_s,
    c_s,
    a_s,
    u_s,
    ypre,
    sz,
    g_s,
    out_s,
    dt32,
    rowb,
    rows,
    wdev,
    colb,
    csel,
    bsel,
    bt,
    state,
    s_mine,
    s_part,
    d_mine,
    d_part,
    c_send,
    q1,
    dc_send,
    dq1,
    t_send,
    q2,
    h_mine,
    h_part,
    hb,
    pbuf,
    rx,
    qsum,
    ry,
    lbuf,
    ss_mine,
    ss_rx,
    ss_x,
    ss_ry,
    colscale,
    in_sem,
    out_sem,
    sa_sem,
    ra_sem,
    sx_sem,
    rx_sem,
    sy_sem,
    ry_sem,
    sgy_sem,
    rgy_sem,
    sgx_sem,
    rgx_sem,
    ssx_s,
    ssx_r,
    ssy_s,
    ssy_r,
):
    tok = x_s.shape[0]
    nc = tok // L
    nh = dt_ref.shape[0]
    qt = tok // xn
    pt = qt // yn
    rank = lax.axis_index("seq")
    hd = lax.axis_index("head")
    core = lax.rem(rank, 2)
    z = rank // 2
    nz = seq_n // 2
    mx = hd // yn
    my = lax.rem(hd, yn)
    group = hd * nh // (SPACE_HEADS // GROUPS)

    def seq_dev(dz):
        return (lax.rem(z + dz + nz, nz) * 2 + core, hd)

    partner = (z * 2 + 1 - core, hd)

    def x_dev(i):
        return (rank, lax.rem(mx + i, xn) * yn + my)

    def y_dev(i):
        return (rank, mx * yn + lax.rem(my + i, yn))

    chain = nz > 4
    peers = [partner]
    if chain:
        peers += [seq_dev(d) for d in (1, -1, 2, -2)]
    peers += [x_dev(i) for i in range(1, xn)]
    peers += [y_dev(i) for i in range(1, yn)]
    barrier = pltpu.get_barrier_semaphore()
    for peer in peers:
        pl.semaphore_signal(barrier, inc=1, device_id=peer, device_id_type=MESH)

    def load(src, dst, k):
        copy = pltpu.make_async_copy(src, dst, in_sem.at[k])
        copy.start()
        return copy

    b_in = load(b_hbm, b_s, 0)
    x_in = load(x_hbm, x_s, 1)
    c_in = load(c_hbm, c_s, 2)
    z_in = load(z_hbm, z_s, 3)
    a_in = [load(down_hbm.at[k], a_s.at[:, pl.ds(k * 128, 128)], 4 + k) for k in range(4)]
    u_in = load(up_hbm, u_s, 8)

    for c in range(nc):
        dt32[pl.ds(c * nh, nh), :] = dt_ref[:, pl.ds(c * L, L)]
    shape = (nc * nh, L)
    rid = lax.broadcasted_iota(jnp.int32, shape, 0)
    lane = lax.broadcasted_iota(jnp.int32, shape, 1)
    head_of = rid % nh
    chunk_of = rid // nh
    raw = dt32[...]
    dt = jnp.maximum(raw, 0.0) + jnp.log1p(jnp.exp(-jnp.abs(raw)))
    alog = jnp.full(shape, a_log[0], F32)
    for h in range(1, nh):
        alog = jnp.where(head_of == h, a_log[h], alog)
    ld = dt * -jnp.exp(alog)
    ki = lax.broadcasted_iota(jnp.int32, (L, L), 0)
    kj = lax.broadcasted_iota(jnp.int32, (L, L), 1)
    cum = mm(ld, (ki <= kj).astype(F32), HIGHEST)
    suf = mm(ld, (ki > kj).astype(F32), HIGHEST)
    tot = jnp.broadcast_to(jnp.sum(ld, axis=1, keepdims=True), shape)

    def down(v, k):
        return jnp.where(rid >= k, pltpu.roll(v, k, 0), 0.0)

    def up(v, k):
        return jnp.where(rid < nc * nh - k, pltpu.roll(v, nc * nh - k, 0), 0.0)

    pre, post = (down(tot, nh), up(tot, nh))
    step = nh
    while step < nc * nh:
        pre = pre + down(pre, step)
        post = post + up(post, step)
        step *= 2
    starts, first = ([], jnp.int32(0))
    for k in range(doc_len.shape[0]):
        starts.append(first)
        first = first + doc_len[k]
    base = rank * tok

    def docs(t):
        total = None
        for s in starts:
            one = (t >= s).astype(jnp.int32)
            total = one if total is None else total + one
        return total

    n_t = docs(base + chunk_of * L + lane)
    n_cs = docs(base + chunk_of * L - 1)
    n_ce = docs(base + chunk_of * L + (L - 1))
    n_bs = docs(base + 0 * chunk_of - 1)
    n_be = docs(base + 0 * chunk_of + (tok - 1))
    lang = jnp.zeros(shape, jnp.int32)
    for k in range(doc_lang.shape[0]):
        lang = jnp.where(n_t == k + 1, doc_lang[k], lang)

    def keep(cond, v):
        return jnp.where(cond, v, 0.0)

    carry = keep(n_t == n_cs, jnp.exp(cum))
    enter = keep(n_t == n_bs, jnp.exp(pre + cum))
    w_dev = keep(n_t == n_be, jnp.exp(suf + post)) * dt
    w_chunk = keep(n_t == n_ce, jnp.exp(suf)) * dt
    kept = keep(n_ce == n_cs, jnp.exp(tot))
    through = keep(n_be == n_bs, jnp.exp(pre + tot))
    n_f = n_t.astype(F32)
    lang_f = lang.astype(F32)
    for c in range(nc):
        own = slice(c * nh, (c + 1) * nh)
        for k, v in enumerate((cum, carry, enter)):
            rowb[c, k * nh : (k + 1) * nh, :] = v[own]
        rowb[c, 12:13, :] = n_f[c * nh : c * nh + 1]
        rowb[c, 13:14, :] = lang_f[c * nh : c * nh + 1]
        rowb[c, 14:16, :] = jnp.zeros((2, L), F32)
        for k, v in enumerate((cum, dt, w_chunk, kept)):
            rows[c, k * nh : (k + 1) * nh, :] = v[own]
        rows[c, 16:17, :] = n_f[c * nh : c * nh + 1]
        wdev[:, c * L : (c + 1) * L] = w_dev[own]
    for h in range(nh):
        r = (nc - 1) * nh + h
        d_mine[h // 2, :, (h % 2) * 128 : (h % 2 + 1) * 128] = jnp.broadcast_to(
            through[r : r + 1], (8, L)
        )
    cols = jnp.transpose(rowb[...].reshape(nc * 16, L))
    for c in range(nc):
        colb[c, :, 0:16] = cols[:, c * 16 : (c + 1) * 16]

    pr = lax.broadcasted_iota(jnp.int32, (L, L * GROUPS), 0)
    pc = lax.broadcasted_iota(jnp.int32, (L, L * GROUPS), 1)
    pick = (pc == pr * GROUPS + group).astype(BF16)
    b_in.wait()
    for c in range(nc):
        part = mm(pick, b_s[c * L * GROUPS : (c + 1) * L * GROUPS, :])
        bsel[c] = part.astype(BF16)
        bt[:, c * L : (c + 1) * L] = jnp.transpose(part)
    x_in.wait()
    for h in range(nh):
        lhs = (bt[...] * wdev[h : h + 1, :]).astype(BF16)
        s_mine[h // 2, :, (h % 2) * 128 : (h % 2 + 1) * 128] = mm(
            lhs, x_s[:, h * 128 : (h + 1) * 128]
        )
    pl.semaphore_wait(barrier, len(peers))

    def send(src, dst, s_sem, r_sem, dev):
        copy = pltpu.make_async_remote_copy(
            src_ref=src, dst_ref=dst, send_sem=s_sem, recv_sem=r_sem,
            device_id=dev, device_id_type=MESH,
        )
        copy.start()
        return copy

    other = 1 - core
    pair = [
        send(s_mine.at[other], s_part.at[other], sa_sem.at[0], ra_sem.at[0], partner),
        send(d_mine, d_part, sa_sem.at[1], ra_sem.at[1], partner),
        send(s_mine.at[core], s_part.at[core], sa_sem.at[2], ra_sem.at[2], partner),
    ]

    c_in.wait()
    for c in range(nc):
        csel[c] = mm(pick, c_s[c * L * GROUPS : (c + 1) * L * GROUPS, :]).astype(BF16)

    pair[0].wait_recv()
    pair[1].wait_recv()
    is_second = core == 1
    if chain:
        sm, sp = s_mine[core], s_part[core]
        dm, dp = d_mine[core][0:1], d_part[core][0:1]
        earlier = jnp.where(is_second, sp, sm)
        latter = jnp.where(is_second, sm, sp)
        d_latter = jnp.where(is_second, dm, dp)
        chip_s = d_latter * earlier + latter
        chip_d = dm * dp
        h_mine[...] = chip_s
        c_send[...] = chip_s.astype(BF16)
        dc_send[...] = jnp.broadcast_to(chip_d, dc_send.shape)
        ring = [
            send(c_send, q1, sa_sem.at[3], ra_sem.at[3], seq_dev(1)),
            send(dc_send, dq1, sa_sem.at[4], ra_sem.at[4], seq_dev(1)),
        ]

    state[...] = jnp.zeros_like(state)
    lower = ki >= kj

    def chunk(c, carry_in):
        at = pl.multiple_of(c * L, L)
        col = colb[c]
        row = rows[c]
        cc = csel[c]
        gram = nt(cc, bsel[c])
        same = col[:, 12:13] == row[16:17]
        gram = jnp.where(same & lower, gram, 0.0)
        cf = cc.astype(F32)
        btc = bt[:, pl.ds(at, L)]
        for h in range(nh):
            hs = slice(h * 128, (h + 1) * 128)
            gap = jnp.minimum(col[:, h : h + 1] - row[h : h + 1], 0.0)
            w = (gram * jnp.exp(gap) * row[nh + h : nh + h + 1]).astype(BF16)
            xh = x_s[pl.ds(at, L), hs]
            st = state[h]
            cw = (cf * col[:, nh + h : nh + h + 1]).astype(BF16)
            y = mm(w, xh) + mm(cw, st.astype(BF16)) + d_skip[h] * xh.astype(F32)
            ypre[pl.ds(at, L), hs] = y
            new = (btc * row[2 * nh + h : 2 * nh + h + 1]).astype(BF16)
            state[h] = st * row[3 * nh + h : 3 * nh + h + 1] + mm(new, xh)
        return carry_in

    def silu(c, carry_in):
        at = pl.multiple_of(c * L, L)
        for h in range(nh):
            hs = slice(h * 128, (h + 1) * 128)
            v = z_s[pl.ds(at, L), hs].astype(F32)
            sz[pl.ds(at, L), hs] = v / (1.0 + jnp.exp(-v))
        return carry_in

    cut = nc // 2
    lax.fori_loop(0, cut, chunk, 0)

    if chain:
        ring[0].wait_recv()
        ring[1].wait_recv()
        from1 = jnp.where(z >= 1, q1[...].astype(F32), 0.0)
        t_send[...] = (h_mine[...] + chip_d * from1).astype(BF16)
        far = send(t_send, q2, sa_sem.at[5], ra_sem.at[5], seq_dev(2))
    z_in.wait()
    lax.fori_loop(cut, nc, chunk, 0)
    lax.fori_loop(0, nc // 2, silu, 0)
    pair[2].wait_recv()
    for copy in pair:
        copy.wait_send()
    if chain:
        far.wait_recv()
        from1 = jnp.where(z >= 1, q1[...].astype(F32), 0.0)
        from2 = jnp.where(z >= 2, q2[...].astype(F32), 0.0)
        h_mine[...] = from1 + dq1[0:1, :] * from2
        back = send(h_mine, h_part, sa_sem.at[6], ra_sem.at[6], partner)
        lax.fori_loop(nc // 2, nc, silu, 0)
        back.wait_recv()
        for half in range(2):
            inc = jnp.where(core == half, h_mine[...], h_part[...])
            second = d_part[half][0:1] * inc + s_part[half]
            hb[half] = jnp.where(is_second, second, inc).astype(BF16)
        back.wait_send()
        far.wait_send()
        for copy in ring:
            copy.wait_send()
    else:
        lax.fori_loop(nc // 2, nc, silu, 0)
        for half in range(2):
            hb[half] = jnp.where(is_second, s_part[half], 0.0).astype(BF16)

    for copy in a_in:
        copy.wait()
    per_q = qt // L
    one8 = jnp.ones((8, L), F32)

    def gate(q):
        def body(i, carry_in):
            c = q * per_q + i
            at = pl.multiple_of(c * L, L)
            col = colb[c]
            cc = csel[c]
            sq = None
            for h in range(nh):
                hs = slice(h * 128, (h + 1) * 128)
                hw = hb[h // 2, :, (h % 2) * 128 : (h % 2 + 1) * 128]
                ent = mm(cc, hw) * col[:, 2 * nh + h : 2 * nh + h + 1]
                gated = (ypre[pl.ds(at, L), hs] + ent) * sz[pl.ds(at, L), hs]
                sq = gated * gated if sq is None else sq + gated * gated
                g_s[pl.ds(at, L), hs] = (gated * gain_ref[0:1, hs]).astype(BF16)
            ss_mine[pl.ds(c, 1), :] = nt(one8, sq, HIGHEST)[0:1]
            g = g_s[pl.ds(at, L), :]
            lg = col[:, 13:14]
            picked = None
            for k in range(0, 4, 2):
                two = mm(g, a_s[:, k * 128 : (k + 2) * 128])
                for j in range(2):
                    one = jnp.where(lg == float(k + j), two[:, j * 128 : (j + 1) * 128], 0.0)
                    picked = one if picked is None else picked + one
            pbuf[q, pl.ds(pl.multiple_of(i * L, L), L), :] = picked.astype(BF16)
            return carry_in

        lax.fori_loop(0, per_q, body, 0)

    sends = []
    order = sorted(range(1, xn), key=lambda i: -min(i, xn - i))
    for i in order:
        q = lax.rem(mx + i, xn)
        gate(q)
        sends.append(send(pbuf.at[q], rx.at[mx], sx_sem.at[i], rx_sem.at[mx], x_dev(i)))
    gate(mx)
    for i in order:
        sends.append(send(ss_mine, ss_rx.at[mx], ssx_s.at[i], ssx_r.at[mx], x_dev(i)))

    def arrived(dst, sem):
        pltpu.make_async_remote_copy(
            src_ref=dst, dst_ref=dst, send_sem=in_sem.at[0], recv_sem=sem,
            device_id=partner, device_id_type=MESH,
        ).wait_recv()

    total = pbuf[mx].astype(F32)
    for i in order[::-1]:
        src = lax.rem(mx + i, xn)
        arrived(rx.at[src], rx_sem.at[src])
        total = total + rx[src].astype(F32)
    qsum[...] = total.astype(BF16).reshape(qsum.shape)
    y_order = sorted(range(1, yn), key=lambda i: -min(i, yn - i))
    for i in y_order:
        p = lax.rem(my + i, yn)
        sends.append(send(qsum.at[p], ry.at[my], sy_sem.at[i], ry_sem.at[my], y_dev(i)))
    ss = ss_mine[...]
    for i in order[::-1]:
        src = lax.rem(mx + i, xn)
        arrived(ss_rx.at[src], ssx_r.at[src])
        ss = ss + ss_rx[src]
    ss_x[...] = ss
    for i in y_order:
        sends.append(send(ss_x, ss_ry.at[my], ssy_s.at[i], ssy_r.at[my], y_dev(i)))
    piece = qsum[my].astype(F32)
    for i in y_order[::-1]:
        src = lax.rem(my + i, yn)
        arrived(ry.at[src], ry_sem.at[src])
        piece = piece + ry[src].astype(F32)
    lbuf[mx, my] = piece.astype(BF16)
    for i in y_order:
        sends.append(send(lbuf.at[mx, my], lbuf.at[mx, my], sgy_sem.at[i], rgy_sem.at[my], y_dev(i)))

    def forward(p, k):
        for i in order:
            sends.append(
                send(lbuf.at[mx, p], lbuf.at[mx, p], sgx_sem.at[i, k], rgx_sem.at[mx], x_dev(i))
            )

    forward(my, 0)

    for i in y_order[::-1]:
        src = lax.rem(my + i, yn)
        arrived(ss_ry.at[src], ssy_r.at[src])
        ss = ss + ss_ry[src]
    scale = lax.rsqrt(ss / (SPACE_HEADS * HEAD_DIM) + 1e-05)
    eye = ki == kj
    for c in range(nc):
        spread = jnp.broadcast_to(scale[c : c + 1], (L, L))
        one = jnp.sum(jnp.where(eye, spread, 0.0), axis=1, keepdims=True)
        colscale[c] = jnp.broadcast_to(one, (L, L))

    for i in y_order[::-1]:
        p = lax.rem(my + i, yn)
        arrived(lbuf.at[mx, p], rgy_sem.at[p])
        forward(p, i)

    u_in.wait()

    def finish(q):
        def body(i, carry_in):
            c = q * per_q + i
            at = pl.multiple_of(c * L, L)
            lg = colb[c][:, 13:14]
            if pt > L:
                low = lbuf[q, 0, pl.ds(pl.multiple_of(i * L, L), L)].astype(F32)
            else:
                per = L // pt
                low = lbuf[q, pl.ds(i * per, per)].reshape(L, 128).astype(F32)
            sel = jnp.concatenate(
                [jnp.where(lg == float(k), low, 0.0).astype(BF16) for k in range(4)], axis=1
            )
            scl = colscale[c]
            for h in range(0, nh, 2):
                lift = mm(sel, u_s[:, h * 128 : (h + 2) * 128])
                for j in range(2):
                    hs = slice((h + j) * 128, (h + j + 1) * 128)
                    val = g_s[pl.ds(at, L), hs].astype(F32) + lift[:, j * 128 : (j + 1) * 128]
                    out_s[pl.ds(at, L), hs] = (val * scl).astype(BF16)
            return carry_in

        lax.fori_loop(0, per_q, body, 0)
        at = pl.multiple_of(q * qt, qt)
        copy = pltpu.make_async_copy(
            out_s.at[pl.ds(at, qt), :], out_hbm.at[pl.ds(at, qt), :], out_sem.at[q]
        )
        copy.start()
        return copy

    outs = [finish(mx)]
    for i in order[::-1]:
        q = lax.rem(mx + i, xn)
        arrived(lbuf.at[q], rgx_sem.at[q])
        outs.append(finish(q))
    for copy in sends:
        copy.wait_send()
    for copy in outs:
        copy.wait()


def per_device(seq_n, xn, yn, x_in, z_gate, b_input, c_input, dt_raw, a_log, d_skip, norm_gain,
               doc_lengths, doc_lang, adapt_down, adapt_up):
    tok, feat = x_in.shape
    nh = dt_raw.shape[0]
    nc = tok // L
    qt = tok // xn
    pt = qt // yn
    half = feat // 2
    dma = pltpu.SemaphoreType.DMA
    vm = pltpu.VMEM
    scratch = [
        vm((tok, feat), BF16),
        vm((tok, feat), BF16),
        vm((tok * GROUPS, 128), BF16),
        vm((tok * GROUPS, 128), BF16),
        vm((feat, 512), BF16),
        vm((512, feat), BF16),
        vm((tok, feat), F32),
        vm((tok, feat), F32),
        vm((tok, feat), BF16),
        vm((tok, feat), BF16),
        vm((nc * nh, L), F32),
        vm((nc, 16, L), F32),
        vm((nc, 24, L), F32),
        vm((nh, tok), F32),
        vm((nc, L, L), F32),
        vm((nc, L, L), BF16),
        vm((nc, L, L), BF16),
        vm((L, tok), F32),
        vm((nh, 128, 128), F32),
        vm((2, 128, half), F32),
        vm((2, 128, half), F32),
        vm((2, 8, half), F32),
        vm((2, 8, half), F32),
        vm((128, half), BF16),
        vm((128, half), BF16),
        vm((8, half), F32),
        vm((8, half), F32),
        vm((128, half), BF16),
        vm((128, half), BF16),
        vm((128, half), F32),
        vm((128, half), F32),
        vm((2, 128, half), BF16),
        vm((xn, qt, 128), BF16),
        vm((xn, qt, 128), BF16),
        vm((yn, pt, 128), BF16),
        vm((yn, pt, 128), BF16),
        vm((xn, yn, pt, 128), BF16),
        vm((nc, L), F32),
        vm((xn, nc, L), F32),
        vm((nc, L), F32),
        vm((yn, nc, L), F32),
        vm((nc, L, L), F32),
        dma((9,)),
        dma((xn,)),
        dma((7,)),
        dma((7,)),
        dma((xn,)),
        dma((xn,)),
        dma((yn,)),
        dma((yn,)),
        dma((yn,)),
        dma((yn,)),
        dma((xn, yn)),
        dma((xn,)),
        dma((xn,)),
        dma((xn,)),
        dma((yn,)),
        dma((yn,)),
    ]
    smem = pl.BlockSpec(memory_space=pltpu.SMEM)
    vmem = pl.BlockSpec(memory_space=pltpu.VMEM)
    hbm = pl.BlockSpec(memory_space=pl.ANY)
    return pl.pallas_call(
        functools.partial(kernel_body, seq_n, xn, yn),
        out_shape=jax.ShapeDtypeStruct((tok, feat), BF16),
        in_specs=[smem] * 4 + [vmem] * 2 + [hbm] * 6,
        out_specs=hbm,
        scratch_shapes=scratch,
        compiler_params=pltpu.CompilerParams(
            collective_id=0, has_side_effects=True, vmem_limit_bytes=48 * 1024 * 1024
        ),
    )(
        doc_lengths,
        doc_lang,
        a_log,
        d_skip,
        dt_raw,
        norm_gain.reshape(1, feat),
        x_in,
        z_gate,
        b_input.reshape(tok * GROUPS, 128),
        c_input.reshape(tok * GROUPS, 128),
        adapt_down,
        adapt_up.reshape(512, feat),
    )


def solution(mesh):
    seq_n, head_n = mesh.shape["seq"], mesh.shape["head"]
    xn = 4 if head_n == 32 else min(2, head_n)
    placed = (
        P("seq", "head"),
        P("seq", "head"),
        P("seq", None, None),
        P("seq", None, None),
        P("head", "seq"),
        P("head"),
        P("head"),
        P("head"),
        P(),
        P(),
        P(None, "head", None),
        P(None, None, "head"),
    )
    return jax.shard_map(
        functools.partial(per_device, seq_n, xn, head_n // xn),
        mesh=mesh, in_specs=placed, out_specs=P("seq", "head"), check_vma=False,
    )
```

```python
import functools

import jax
import jax.numpy as jnp
from jax import lax
from jax.experimental import pallas as pl
from jax.experimental.pallas import tpu as pltpu
from jax.sharding import PartitionSpec as P

SPACE_HEADS = 128
HEAD_DIM = 128
GROUPS = 8
L = 128
MESH = pl.DeviceIdType.MESH
F32 = jnp.float32
BF16 = jnp.bfloat16
HIGHEST = lax.Precision.HIGHEST


def nt(a, b, precision=None):
    return lax.dot_general(
        a, b, (((1,), (1,)), ((), ())), preferred_element_type=F32, precision=precision
    )


def mm(a, b, precision=None):
    return jnp.dot(a, b, preferred_element_type=F32, precision=precision)


def kernel_body(
    seq_n,
    xn,
    yn,
    doc_len_hbm,
    doc_lang_hbm,
    a_log_hbm,
    d_skip_hbm,
    dt_hbm,
    gain_hbm,
    x_hbm,
    z_hbm,
    b_hbm,
    c_hbm,
    down_hbm,
    up_hbm,
    out_hbm,
    doc_len,
    doc_lang,
    a_log,
    d_skip,
    dt_ref,
    gain_ref,
    gain_s,
    x_s,
    z_s,
    b_s,
    c_s,
    a_s,
    u_s,
    ypre,
    sz,
    g_s,
    out_s,
    sqs,
    pick_s,
    dt32,
    rowb,
    rows,
    wdev,
    colb,
    csel,
    bsel,
    bt,
    state,
    s_mine,
    s_part,
    d_mine,
    d_part,
    c_send,
    q1,
    dc_send,
    dq1,
    t_send,
    q2,
    h_mine,
    h_send,
    h_part,
    hb,
    pbuf,
    rx,
    qsum,
    ry,
    lbuf,
    ss_mine,
    ss_rx,
    ss_x,
    ss_ry,
    colscale,
    in_sem,
    out_sem,
    sa_sem,
    ra_sem,
    sx_sem,
    rx_sem,
    sy_sem,
    ry_sem,
    sgy_sem,
    rgy_sem,
    sgx_sem,
    rgx_sem,
    ssx_s,
    ssx_r,
    ssy_s,
    ssy_r,
):
    tok = x_s.shape[1]
    nc = tok // L
    nh = dt_ref.shape[0]
    qt = tok // xn
    pt = qt // yn
    rank = lax.axis_index("seq")
    hd = lax.axis_index("head")
    core = lax.rem(rank, 2)
    z = rank // 2
    nz = seq_n // 2
    mx = hd // yn
    my = lax.rem(hd, yn)
    group = hd * nh // (SPACE_HEADS // GROUPS)

    def seq_dev(dz):
        return (lax.rem(z + dz + nz, nz) * 2 + core, hd)

    partner = (z * 2 + 1 - core, hd)

    def x_dev(i):
        return (rank, lax.rem(mx + i, xn) * yn + my)

    def y_dev(i):
        return (rank, mx * yn + lax.rem(my + i, yn))

    chain = nz > 4
    peers = [partner]
    if chain:
        peers += [seq_dev(d) for d in (1, -1, 2, -2)]
    peers += [x_dev(i) for i in range(1, xn)]
    peers += [y_dev(i) for i in range(1, yn)]
    barrier = pltpu.get_barrier_semaphore()
    for peer in peers:
        pl.semaphore_signal(barrier, inc=1, device_id=peer, device_id_type=MESH)

    def load(src, dst, k):
        copy = pltpu.make_async_copy(src, dst, in_sem.at[k])
        copy.start()
        return copy

    small = [
        load(src, dst, 9 + k)
        for k, (src, dst) in enumerate(
            (
                (dt_hbm, dt_ref),
                (a_log_hbm, a_log),
                (doc_len_hbm, doc_len),
                (doc_lang_hbm, doc_lang),
                (d_skip_hbm, d_skip),
                (gain_hbm, gain_ref),
            )
        )
    ]
    def load_pair(src, dst, k):
        return [
            load(src.at[:, j, group // 2], dst.at[:, 2 * j : 2 * j + 2, :], k + j)
            for j in range(8)
        ]

    b_in = load_pair(b_hbm, b_s, 15)
    x_in = [load(x_hbm.at[:, pl.ds(k * 256, 256)], x_s.at[k], k) for k in range(2)]

    for copy in small:
        copy.wait()
    for c in range(nc):
        dt32[pl.ds(c * nh, nh), :] = dt_ref[:, pl.ds(c * L, L)]
    shape = (nc * nh, L)
    rid = lax.broadcasted_iota(jnp.int32, shape, 0)
    lane = lax.broadcasted_iota(jnp.int32, shape, 1)
    head_of = rid & (nh - 1)
    chunk_of = lax.shift_right_logical(rid, nh.bit_length() - 1)
    raw = dt32[...]
    dt = jnp.maximum(raw, 0.0) + jnp.log1p(jnp.exp(-jnp.abs(raw)))
    alog = jnp.full(shape, a_log[0], F32)
    for h in range(1, nh):
        alog = jnp.where(head_of == h, a_log[h], alog)
    ld = dt * -jnp.exp(alog)
    ki = lax.broadcasted_iota(jnp.int32, (L, L), 0)
    kj = lax.broadcasted_iota(jnp.int32, (L, L), 1)
    cum = mm(ld, (ki <= kj).astype(F32), HIGHEST)
    suf = mm(ld, (ki > kj).astype(F32), HIGHEST)
    tot = jnp.broadcast_to(jnp.sum(ld, axis=1, keepdims=True), shape)

    def down(v, k):
        return jnp.where(rid >= k, pltpu.roll(v, k, 0), 0.0)

    def up(v, k):
        return jnp.where(rid < nc * nh - k, pltpu.roll(v, nc * nh - k, 0), 0.0)

    pre, post = (down(tot, nh), up(tot, nh))
    step = nh
    while step < nc * nh:
        pre = pre + down(pre, step)
        post = post + up(post, step)
        step *= 2
    starts, first = ([], jnp.int32(0))
    for k in range(doc_len.shape[0]):
        starts.append(first)
        first = first + doc_len[k]
    base = rank * tok

    def docs(t):
        total = None
        for s in starts:
            one = (t >= s).astype(jnp.int32)
            total = one if total is None else total + one
        return total

    n_t = docs(base + chunk_of * L + lane)
    n_cs = docs(base + chunk_of * L - 1)
    n_ce = docs(base + chunk_of * L + (L - 1))
    n_bs = docs(base + 0 * chunk_of - 1)
    n_be = docs(base + 0 * chunk_of + (tok - 1))
    lang = jnp.zeros(shape, jnp.int32)
    for k in range(doc_lang.shape[0]):
        lang = jnp.where(n_t == k + 1, doc_lang[k], lang)

    def keep(cond, v):
        return jnp.where(cond, v, 0.0)

    carry = keep(n_t == n_cs, jnp.exp(cum))
    enter = keep(n_t == n_bs, jnp.exp(pre + cum))
    w_dev = keep(n_t == n_be, jnp.exp(suf + post)) * dt
    w_chunk = keep(n_t == n_ce, jnp.exp(suf)) * dt
    kept = keep(n_ce == n_cs, jnp.exp(tot))
    through = keep(n_be == n_bs, jnp.exp(pre + tot))
    n_f = n_t.astype(F32)
    lang_f = lang.astype(F32)
    for c in range(nc):
        own = slice(c * nh, (c + 1) * nh)
        for k, v in enumerate((cum, carry, enter)):
            rowb[c, k * nh : (k + 1) * nh, :] = v[own]
        rowb[c, 12:13, :] = n_f[c * nh : c * nh + 1]
        rowb[c, 13:14, :] = lang_f[c * nh : c * nh + 1]
        rowb[c, 14:16, :] = jnp.zeros((2, L), F32)
        for k, v in enumerate((cum, dt, w_chunk, kept)):
            rows[c, k * nh : (k + 1) * nh, :] = v[own]
        rows[c, 16:17, :] = n_f[c * nh : c * nh + 1]
        wdev[:, c * L : (c + 1) * L] = w_dev[own]
    for h in range(nh):
        r = (nc - 1) * nh + h
        d_mine[h] = jnp.broadcast_to(through[r : r + 1], (8, L))
    for k in range(2):
        gain_s[k] = jnp.broadcast_to(gain_ref[0:1, k * 256 : (k + 1) * 256], (8, 256))
    cols = jnp.transpose(rowb[...].reshape(nc * 16, L))
    for c in range(nc):
        colb[c * L : (c + 1) * L, 0:16] = cols[:, c * 16 : (c + 1) * 16]

    pr = lax.broadcasted_iota(jnp.int32, (L, L * 2), 0)
    pc = lax.broadcasted_iota(jnp.int32, (L, L * 2), 1)
    pick = (pc == pr * 2 + lax.rem(group, 2)).astype(BF16)
    for copy in b_in:
        copy.wait()
    c_in = load_pair(c_hbm, c_s, 23)
    z_in = [load(z_hbm.at[:, pl.ds(k * 256, 256)], z_s.at[k], 2 + k) for k in range(2)]
    a_in = [
        load(
            down_hbm.at[k % 4, pl.ds(k // 4 * 256, 256), :],
            a_s.at[k // 4, :, pl.ds(k % 4 * 128, 128)],
            31 + k,
        )
        for k in range(8)
    ]
    u_in = load(up_hbm, u_s, 8)
    for c in range(nc):
        part = mm(pick, b_s[c * 16 : (c + 1) * 16].reshape(2 * L, 128)).astype(BF16)
        bsel[c * L : (c + 1) * L, :] = part
        bt[:, c * L : (c + 1) * L] = jnp.transpose(part)
    pl.semaphore_wait(barrier, len(peers))

    def send(src, dst, s_sem, r_sem, dev):
        copy = pltpu.make_async_remote_copy(
            src_ref=src, dst_ref=dst, send_sem=s_sem, recv_sem=r_sem,
            device_id=dev, device_id_type=MESH,
        )
        copy.start()
        return copy

    pair = [send(d_mine, d_part, sa_sem.at[0], ra_sem.at[0], partner)]
    for copy in x_in:
        copy.wait()
    other = 1 - core
    for k in range(nh):
        half = other if k < 2 else core
        j = k % 2
        h = half * 2 + j
        lhs = bt[...] * wdev[pl.ds(h, 1), :].astype(BF16)
        s_mine[h] = mm(lhs, x_s[half, :, j * 128 : (j + 1) * 128])
        pair.append(send(s_mine.at[h], s_part.at[h], sa_sem.at[1 + k], ra_sem.at[1 + k], partner))

    for copy in c_in:
        copy.wait()
    for c in range(nc):
        part = mm(pick, c_s[c * 16 : (c + 1) * 16].reshape(2 * L, 128))
        csel[c * L : (c + 1) * L, :] = part.astype(BF16)

    is_second = core == 1
    mine = [core * 2 + j for j in range(2)]
    pair[0].wait_recv()
    ring, chip_d = ([], [])
    if chain:
        for j in range(2):
            chip_d.append(d_mine[mine[j]][0:1] * d_part[mine[j]][0:1])
            dc_send[j] = jnp.broadcast_to(chip_d[j], (8, L))
        ring.append(send(dc_send, dq1, sa_sem.at[5], ra_sem.at[5], seq_dev(1)))
        for j in range(2):
            pair[1 + j].wait_recv()
            sm, sp = (s_mine[mine[j]], s_part[mine[j]])
            earlier = jnp.where(is_second, sp, sm)
            latter = jnp.where(is_second, sm, sp)
            d_latter = jnp.where(is_second, d_mine[mine[j]][0:1], d_part[mine[j]][0:1])
            chip_s = d_latter * earlier + latter
            h_mine[j] = chip_s
            c_send[j] = chip_s.astype(BF16)
            ring.append(
                send(c_send.at[j], q1.at[j], sa_sem.at[6 + j], ra_sem.at[6 + j], seq_dev(1))
            )
    else:
        for j in range(2):
            pair[1 + j].wait_recv()

    state[...] = jnp.zeros_like(state)
    lower = ki >= kj

    def chunk(c):
        at = pl.multiple_of(c * L, L)
        col = colb[pl.ds(at, L), :]
        row = rows[c]
        cc = csel[pl.ds(at, L), :]
        gram = nt(cc, bsel[pl.ds(at, L), :])
        same = col[:, 12:13] == row[16:17]
        gram = jnp.where(same & lower, gram, 0.0)
        cf = cc.astype(F32)
        btc = bt[:, pl.ds(at, L)]
        for h in range(nh):
            half, hs = (h // 2, slice(h % 2 * 128, (h % 2 + 1) * 128))
            gap = jnp.minimum(col[:, h : h + 1] - row[h : h + 1], 0.0)
            w = (gram * jnp.exp(gap) * row[nh + h : nh + h + 1]).astype(BF16)
            xh = x_s[half, pl.ds(at, L), hs]
            st = state[h]
            cw = (cf * col[:, nh + h : nh + h + 1]).astype(BF16)
            y = mm(w, xh) + mm(cw, st.astype(BF16)) + d_skip[h] * xh.astype(F32)
            ypre[half, pl.ds(at, L), hs] = y
            new = btc * row[2 * nh + h : 2 * nh + h + 1].astype(BF16)
            state[h] = st * row[3 * nh + h : 3 * nh + h + 1] + mm(new, xh)

    def chunks(i, carry_in):
        chunk(2 * i)
        chunk(2 * i + 1)
        return carry_in

    def silu(c, carry_in):
        at = pl.multiple_of(c * L, L)
        for half in range(2):
            v = z_s[half, pl.ds(at, L), :].astype(F32)
            sz[half, pl.ds(at, L), :] = v / (1.0 + jnp.exp(-v))
        return carry_in

    cut = nc // 4
    lax.fori_loop(0, cut, chunks, 0)

    far = []
    if chain:
        ring[0].wait_recv()
        for j in range(2):
            ring[1 + j].wait_recv()
            from1 = jnp.where(z >= 1, q1[j].astype(F32), 0.0)
            t_send[j] = (h_mine[j] + chip_d[j] * from1).astype(BF16)
            far.append(
                send(t_send.at[j], q2.at[j], sa_sem.at[8 + j], ra_sem.at[8 + j], seq_dev(2))
            )
    for copy in z_in:
        copy.wait()
    lax.fori_loop(cut, nc // 2, chunks, 0)
    lax.fori_loop(0, nc, silu, 0)
    for copy in a_in:
        copy.wait()
    pair[3].wait_recv()
    pair[4].wait_recv()
    for copy in pair + ring:
        copy.wait_send()

    def entering(inc, h):
        second = d_part[h][0:1] * inc + s_part[h]
        return jnp.where(is_second, second, inc).astype(BF16)

    back = []
    for j in range(2):
        js = slice(j * 128, (j + 1) * 128)
        if chain:
            far[j].wait_recv()
            from1 = jnp.where(z >= 1, q1[j].astype(F32), 0.0)
            from2 = jnp.where(z >= 2, q2[j].astype(F32), 0.0)
            inc = from1 + dq1[j][0:1] * from2
            h_send[j] = inc
            back.append(
                send(h_send.at[j], h_part.at[j], sa_sem.at[10 + j], ra_sem.at[10 + j], partner)
            )
        else:
            inc = jnp.zeros((128, 128), F32)
        hb[core, :, js] = entering(inc, mine[j])

    one8 = jnp.ones((8, L), BF16)

    def gate(q, half, last):
        at = q * qt if isinstance(q, int) else pl.multiple_of(q * qt, qt)
        here = pl.ds(at, qt)
        col = colb[here, :]
        cc = csel[here, :]
        sq = sqs[here, :] if last else None
        picked = pick_s[here, :] if last else None
        for j in range(2):
            js = slice(j * 128, (j + 1) * 128)
            lo = col[:, 2 * nh + j : 2 * nh + j + 1]
            hi = col[:, 2 * nh + 2 + j : 2 * nh + 3 + j]
            ent = mm(cc, hb[half, :, js]) * jnp.where(half == 1, hi, lo)
            gated = (ypre[half, here, js] + ent) * sz[half, here, js]
            sq = gated * gated if sq is None else sq + gated * gated
            g_s[half, here, js] = (gated * gain_s[half, 0:1, js]).astype(BF16)
        lg = col[:, 13:14]
        for k in range(0, 4, 2):
            two = mm(g_s[half, here, :], a_s[half, :, k * 128 : (k + 2) * 128])
            for j in range(2):
                one = jnp.where(lg == float(k + j), two[:, j * 128 : (j + 1) * 128], 0.0)
                picked = one if picked is None else picked + one
        if last:
            sums = nt(one8, sq.astype(BF16))
            for i in range(qt // L):
                ss_mine[pl.ds(q * (qt // L) + i, 1), :] = sums[0:1, i * L : (i + 1) * L]
            pbuf[q] = picked.astype(BF16)
        else:
            sqs[here, :] = sq
            pick_s[here, :] = picked

    for q in range(xn):
        gate(q, core, False)
    for j in range(2):
        if chain:
            back[j].wait_recv()
            inc = h_part[j]
        else:
            inc = jnp.zeros((128, 128), F32)
        hb[other, :, j * 128 : (j + 1) * 128] = entering(inc, other * 2 + j)
    for copy in back + far:
        copy.wait_send()
    sends = []
    order = sorted(range(1, xn), key=lambda i: -min(i, xn - i))
    for i in order:
        q = lax.rem(mx + i, xn)
        gate(q, other, True)
        sends.append(send(pbuf.at[q], rx.at[mx], sx_sem.at[i], rx_sem.at[mx], x_dev(i)))
    gate(mx, other, True)
    for i in order:
        sends.append(send(ss_mine, ss_rx.at[mx], ssx_s.at[i], ssx_r.at[mx], x_dev(i)))

    def arrived(dst, sem):
        pltpu.make_async_remote_copy(
            src_ref=dst, dst_ref=dst, send_sem=in_sem.at[0], recv_sem=sem,
            device_id=partner, device_id_type=MESH,
        ).wait_recv()

    total = pbuf[mx].astype(F32)
    for i in order[::-1]:
        src = lax.rem(mx + i, xn)
        arrived(rx.at[src], rx_sem.at[src])
        total = total + rx[src].astype(F32)
    qsum[...] = total.astype(BF16).reshape(qsum.shape)
    y_order = sorted(range(1, yn), key=lambda i: -min(i, yn - i))
    for i in y_order:
        p = lax.rem(my + i, yn)
        sends.append(send(qsum.at[p], ry.at[my], sy_sem.at[i], ry_sem.at[my], y_dev(i)))
    ss = ss_mine[...]
    for i in order[::-1]:
        src = lax.rem(mx + i, xn)
        arrived(ss_rx.at[src], ssx_r.at[src])
        ss = ss + ss_rx[src]
    ss_x[...] = ss
    for i in y_order:
        sends.append(send(ss_x, ss_ry.at[my], ssy_s.at[i], ssy_r.at[my], y_dev(i)))
    piece = qsum[my].astype(F32)
    for i in y_order[::-1]:
        src = lax.rem(my + i, yn)
        arrived(ry.at[src], ry_sem.at[src])
        piece = piece + ry[src].astype(F32)
    lbuf[mx, my] = piece.astype(BF16)
    for i in y_order:
        sends.append(send(lbuf.at[mx, my], lbuf.at[mx, my], sgy_sem.at[i], rgy_sem.at[my], y_dev(i)))

    def forward(p, k):
        for i in order:
            sends.append(
                send(lbuf.at[mx, p], lbuf.at[mx, p], sgx_sem.at[i, k], rgx_sem.at[mx], x_dev(i))
            )

    forward(my, 0)

    for i in y_order[::-1]:
        src = lax.rem(my + i, yn)
        arrived(ss_ry.at[src], ssy_r.at[src])
        ss = ss + ss_ry[src]
    scale = lax.rsqrt(ss / (SPACE_HEADS * HEAD_DIM) + 1e-05)
    eye = ki == kj
    for c in range(nc):
        spread = jnp.broadcast_to(scale[c : c + 1], (L, L))
        one = jnp.sum(jnp.where(eye, spread, 0.0), axis=1, keepdims=True)
        colscale[c * L : (c + 1) * L, :] = jnp.broadcast_to(one, (L, L))

    for i in y_order[::-1]:
        p = lax.rem(my + i, yn)
        arrived(lbuf.at[mx, p], rgy_sem.at[p])
        forward(p, i)

    u_in.wait()

    def finish(q):
        at = pl.multiple_of(q * qt, qt)
        here = pl.ds(at, qt)
        lg = colb[here, 13:14]
        low = lbuf[q].reshape(qt, 128)
        sel = jnp.concatenate(
            [jnp.where(lg == float(k), low, jnp.zeros_like(low)) for k in range(4)], axis=1
        )
        scl = colscale[here, :]
        for h in range(0, nh, 2):
            lift = mm(sel, u_s[:, h * 128 : (h + 2) * 128])
            for j in range(2):
                hs = slice((h + j) * 128, (h + j + 1) * 128)
                val = g_s[h // 2, here, j * 128 : (j + 1) * 128].astype(F32) + lift[:, j * 128 : (j + 1) * 128]
                out_s[here, hs] = (val * scl).astype(BF16)
        copy = pltpu.make_async_copy(
            out_s.at[here, :], out_hbm.at[here, :], out_sem.at[q]
        )
        copy.start()
        return copy

    outs = [finish(mx)]
    for i in order[::-1]:
        q = lax.rem(mx + i, xn)
        arrived(lbuf.at[q], rgx_sem.at[q])
        outs.append(finish(q))
    for copy in sends:
        copy.wait_send()
    for copy in outs:
        copy.wait()


def per_device(seq_n, xn, yn, x_in, z_gate, b_input, c_input, dt_raw, a_log, d_skip, norm_gain,
               doc_lengths, doc_lang, adapt_down, adapt_up):
    tok, feat = x_in.shape
    nh = dt_raw.shape[0]
    nc = tok // L
    qt = tok // xn
    pt = qt // yn
    half = feat // 2
    dma = pltpu.SemaphoreType.DMA
    vm = pltpu.VMEM
    scratch = [
        pltpu.SMEM(doc_lengths.shape, jnp.int32),
        pltpu.SMEM(doc_lang.shape, jnp.int32),
        pltpu.SMEM((nh,), F32),
        pltpu.SMEM((nh,), F32),
        vm((nh, tok), F32),
        vm((1, feat), F32),
        vm((2, 8, half), F32),
        vm((2, tok, half), BF16),
        vm((2, tok, half), BF16),
        vm((tok // 8, 16, 128), BF16),
        vm((tok // 8, 16, 128), BF16),
        vm((2, half, 512), BF16),
        vm((512, feat), BF16),
        vm((2, tok, half), F32),
        vm((2, tok, half), F32),
        vm((2, tok, half), BF16),
        vm((tok, feat), BF16),
        vm((tok, L), F32),
        vm((tok, L), F32),
        vm((nc * nh, L), F32),
        vm((nc, 16, L), F32),
        vm((nc, 24, L), F32),
        vm((nh, tok), F32),
        vm((tok, L), F32),
        vm((tok, L), BF16),
        vm((tok, L), BF16),
        vm((L, tok), BF16),
        vm((nh, 128, 128), F32),
        vm((nh, 128, 128), F32),
        vm((nh, 128, 128), F32),
        vm((nh, 8, L), F32),
        vm((nh, 8, L), F32),
        vm((2, 128, 128), BF16),
        vm((2, 128, 128), BF16),
        vm((2, 8, L), F32),
        vm((2, 8, L), F32),
        vm((2, 128, 128), BF16),
        vm((2, 128, 128), BF16),
        vm((2, 128, 128), F32),
        vm((2, 128, 128), F32),
        vm((2, 128, 128), F32),
        vm((2, 128, half), BF16),
        vm((xn, qt, 128), BF16),
        vm((xn, qt, 128), BF16),
        vm((yn, pt, 128), BF16),
        vm((yn, pt, 128), BF16),
        vm((xn, yn, pt, 128), BF16),
        vm((nc, L), F32),
        vm((xn, nc, L), F32),
        vm((nc, L), F32),
        vm((yn, nc, L), F32),
        vm((tok, L), F32),
        dma((39,)),
        dma((xn,)),
        dma((12,)),
        dma((12,)),
        dma((xn,)),
        dma((xn,)),
        dma((yn,)),
        dma((yn,)),
        dma((yn,)),
        dma((yn,)),
        dma((xn, yn)),
        dma((xn,)),
        dma((xn,)),
        dma((xn,)),
        dma((yn,)),
        dma((yn,)),
    ]
    hbm = pl.BlockSpec(memory_space=pltpu.HBM)
    return pl.pallas_call(
        functools.partial(kernel_body, seq_n, xn, yn),
        out_shape=jax.ShapeDtypeStruct((tok, feat), BF16),
        in_specs=[hbm] * 12,
        out_specs=hbm,
        scratch_shapes=scratch,
        compiler_params=pltpu.CompilerParams(
            collective_id=0, has_side_effects=True, vmem_limit_bytes=60 * 1024 * 1024
        ),
    )(
        doc_lengths,
        doc_lang,
        a_log,
        d_skip,
        dt_raw,
        norm_gain.reshape(1, feat),
        x_in,
        z_gate,
        b_input.reshape(tok // 8, 8, GROUPS // 2, 2, 128),
        c_input.reshape(tok // 8, 8, GROUPS // 2, 2, 128),
        adapt_down,
        adapt_up.reshape(512, feat),
    )


def solution(mesh):
    seq_n, head_n = mesh.shape["seq"], mesh.shape["head"]
    xn = 4 if head_n == 32 else min(2, head_n)
    placed = (
        P("seq", "head"),
        P("seq", "head"),
        P("seq", None, None),
        P("seq", None, None),
        P("head", "seq"),
        P("head"),
        P("head"),
        P("head"),
        P(),
        P(),
        P(None, "head", None),
        P(None, None, "head"),
    )
    return jax.shard_map(
        functools.partial(per_device, seq_n, xn, head_n // xn),
        mesh=mesh, in_specs=placed, out_specs=P("seq", "head"), check_vma=False,
    )
```

```python
import functools

import jax
import jax.numpy as jnp
from jax import lax
from jax.experimental import pallas as pl
from jax.experimental.pallas import tpu as pltpu
from jax.sharding import PartitionSpec as P

SPACE_HEADS = 128
HEAD_DIM = 128
GROUPS = 8
L = 128
MESH = pl.DeviceIdType.MESH
F32 = jnp.float32
BF16 = jnp.bfloat16
HIGHEST = lax.Precision.HIGHEST


def nt(a, b, precision=None):
    return lax.dot_general(
        a, b, (((1,), (1,)), ((), ())), preferred_element_type=F32, precision=precision
    )


def mm(a, b, precision=None):
    return jnp.dot(a, b, preferred_element_type=F32, precision=precision)


def kernel_body(
    seq_n,
    xn,
    yn,
    doc_len_hbm,
    doc_lang_hbm,
    a_log_hbm,
    d_skip_hbm,
    dt_hbm,
    gain_hbm,
    x_hbm,
    z_hbm,
    b_hbm,
    c_hbm,
    down_hbm,
    up_hbm,
    out_hbm,
    doc_len,
    doc_lang,
    a_log,
    d_skip,
    dt_ref,
    gain_ref,
    gain_s,
    x_s,
    z_s,
    b_s,
    c_s,
    a_s,
    u_s,
    ypre,
    sz,
    g_s,
    out_s,
    sqs,
    pick_s,
    dt32,
    rowb,
    rows,
    wdev,
    colb,
    csel,
    bsel,
    bt,
    state,
    s_mine,
    s_part,
    d_mine,
    d_part,
    c_send,
    q1,
    dc_send,
    dq1,
    t_send,
    q2,
    h_mine,
    h_send,
    h_part,
    hb,
    pbuf,
    rx,
    qsum,
    ry,
    lbuf,
    ss_mine,
    ss_rx,
    ss_x,
    ss_ry,
    colscale,
    in_sem,
    out_sem,
    sa_sem,
    ra_sem,
    sx_sem,
    rx_sem,
    sy_sem,
    ry_sem,
    sgy_sem,
    rgy_sem,
    sgx_sem,
    rgx_sem,
    ssx_s,
    ssx_r,
    ssy_s,
    ssy_r,
    ready,
):
    tok = x_s.shape[1]
    nc = tok // L
    nh = dt_ref.shape[0]
    qt = tok // xn
    pt = qt // yn
    rank = lax.axis_index("seq")
    hd = lax.axis_index("head")
    core = lax.rem(rank, 2)
    z = rank // 2
    nz = seq_n // 2
    mx = hd // yn
    my = lax.rem(hd, yn)
    group = hd * nh // (SPACE_HEADS // GROUPS)

    def seq_dev(dz):
        return (lax.rem(z + dz + nz, nz) * 2 + core, hd)

    partner = (z * 2 + 1 - core, hd)

    def x_dev(i):
        return (rank, lax.rem(mx + i, xn) * yn + my)

    def y_dev(i):
        return (rank, mx * yn + lax.rem(my + i, yn))

    chain = nz > 4
    has = {1: z >= 1, 2: z >= 2}
    feeds = {1: z < nz - 1, 2: z < nz - 2}
    peers = [partner]
    peers += [x_dev(i) for i in range(1, xn)]
    peers += [y_dev(i) for i in range(1, yn)]
    barrier = pltpu.get_barrier_semaphore()
    for peer in peers:
        pl.semaphore_signal(barrier, inc=1, device_id=peer, device_id_type=MESH)
    if chain:
        for d in (1, 2):

            @pl.when(feeds[d])
            def _():
                pl.semaphore_signal(barrier, inc=1, device_id=seq_dev(d), device_id_type=MESH)

    def load(src, dst, k):
        copy = pltpu.make_async_copy(src, dst, in_sem.at[k])
        copy.start()
        return copy

    small = [
        load(src, dst, 9 + k)
        for k, (src, dst) in enumerate(
            (
                (dt_hbm, dt_ref),
                (a_log_hbm, a_log),
                (doc_len_hbm, doc_len),
                (doc_lang_hbm, doc_lang),
                (d_skip_hbm, d_skip),
                (gain_hbm, gain_ref),
            )
        )
    ]
    def load_pair(src, dst, k):
        return [
            load(src.at[:, j, group // 2], dst.at[:, 2 * j : 2 * j + 2, :], k + j)
            for j in range(8)
        ]

    b_in = load_pair(b_hbm, b_s, 15)
    x_in = [load(x_hbm.at[:, pl.ds(k * 256, 256)], x_s.at[k], k) for k in range(2)]

    for copy in small:
        copy.wait()
    for c in range(nc):
        dt32[pl.ds(c * nh, nh), :] = dt_ref[:, pl.ds(c * L, L)]
    shape = (nc * nh, L)
    rid = lax.broadcasted_iota(jnp.int32, shape, 0)
    lane = lax.broadcasted_iota(jnp.int32, shape, 1)
    head_of = rid & (nh - 1)
    chunk_of = lax.shift_right_logical(rid, nh.bit_length() - 1)
    raw = dt32[...]
    dt = jnp.maximum(raw, 0.0) + jnp.log1p(jnp.exp(-jnp.abs(raw)))
    alog = jnp.full(shape, a_log[0], F32)
    for h in range(1, nh):
        alog = jnp.where(head_of == h, a_log[h], alog)
    ld = dt * -jnp.exp(alog)
    ki = lax.broadcasted_iota(jnp.int32, (L, L), 0)
    kj = lax.broadcasted_iota(jnp.int32, (L, L), 1)
    cum = mm(ld, (ki <= kj).astype(F32), HIGHEST)
    suf = mm(ld, (ki > kj).astype(F32), HIGHEST)
    tot = jnp.broadcast_to(jnp.sum(ld, axis=1, keepdims=True), shape)

    def down(v, k):
        return jnp.where(rid >= k, pltpu.roll(v, k, 0), 0.0)

    def up(v, k):
        return jnp.where(rid < nc * nh - k, pltpu.roll(v, nc * nh - k, 0), 0.0)

    pre, post = (down(tot, nh), up(tot, nh))
    step = nh
    while step < nc * nh:
        pre = pre + down(pre, step)
        post = post + up(post, step)
        step *= 2
    starts, first = ([], jnp.int32(0))
    for k in range(doc_len.shape[0]):
        starts.append(first)
        first = first + doc_len[k]
    base = rank * tok

    def docs(t):
        total = None
        for s in starts:
            one = (t >= s).astype(jnp.int32)
            total = one if total is None else total + one
        return total

    n_t = docs(base + chunk_of * L + lane)
    n_cs = docs(base + chunk_of * L - 1)
    n_ce = docs(base + chunk_of * L + (L - 1))
    n_bs = docs(base + 0 * chunk_of - 1)
    n_be = docs(base + 0 * chunk_of + (tok - 1))
    lang = jnp.zeros(shape, jnp.int32)
    for k in range(doc_lang.shape[0]):
        lang = jnp.where(n_t == k + 1, doc_lang[k], lang)

    def keep(cond, v):
        return jnp.where(cond, v, 0.0)

    carry = keep(n_t == n_cs, jnp.exp(cum))
    enter = keep(n_t == n_bs, jnp.exp(pre + cum))
    w_dev = keep(n_t == n_be, jnp.exp(suf + post)) * dt
    w_chunk = keep(n_t == n_ce, jnp.exp(suf)) * dt
    kept = keep(n_ce == n_cs, jnp.exp(tot))
    through = keep(n_be == n_bs, jnp.exp(pre + tot))
    n_f = n_t.astype(F32)
    lang_f = lang.astype(F32)
    for c in range(nc):
        own = slice(c * nh, (c + 1) * nh)
        for k, v in enumerate((cum, carry, enter)):
            rowb[c, k * nh : (k + 1) * nh, :] = v[own]
        rowb[c, 12:13, :] = n_f[c * nh : c * nh + 1]
        rowb[c, 13:14, :] = lang_f[c * nh : c * nh + 1]
        rowb[c, 14:16, :] = jnp.zeros((2, L), F32)
        for k, v in enumerate((cum, dt, w_chunk, kept)):
            rows[c, k * nh : (k + 1) * nh, :] = v[own]
        rows[c, 16:17, :] = n_f[c * nh : c * nh + 1]
        wdev[:, c * L : (c + 1) * L] = w_dev[own]
    for h in range(nh):
        r = (nc - 1) * nh + h
        d_mine[h] = jnp.broadcast_to(through[r : r + 1], (8, L))
    for k in range(2):
        gain_s[k] = jnp.broadcast_to(gain_ref[0:1, k * 256 : (k + 1) * 256], (8, 256))
    cols = jnp.transpose(rowb[...].reshape(nc * 16, L))
    for c in range(nc):
        colb[c * L : (c + 1) * L, 0:16] = cols[:, c * 16 : (c + 1) * 16]

    pr = lax.broadcasted_iota(jnp.int32, (L, L * 2), 0)
    pc = lax.broadcasted_iota(jnp.int32, (L, L * 2), 1)
    pick = (pc == pr * 2 + lax.rem(group, 2)).astype(BF16)
    for copy in b_in:
        copy.wait()
    c_in = load_pair(c_hbm, c_s, 23)
    z_in = [load(z_hbm.at[:, pl.ds(k * 256, 256)], z_s.at[k], 2 + k) for k in range(2)]
    a_in = [
        load(
            down_hbm.at[k % 4, pl.ds(k // 4 * 256, 256), :],
            a_s.at[k // 4, :, pl.ds(k % 4 * 128, 128)],
            31 + k,
        )
        for k in range(8)
    ]
    u_in = load(up_hbm, u_s, 8)
    for c in range(nc):
        part = mm(pick, b_s[c * 16 : (c + 1) * 16].reshape(2 * L, 128)).astype(BF16)
        bsel[c * L : (c + 1) * L, :] = part
        bt[:, c * L : (c + 1) * L] = jnp.transpose(part)
    pl.semaphore_wait(barrier, len(peers) + (jnp.minimum(z, 2) if chain else 0))
    if chain:
        for d in (1, 2):

            @pl.when(has[d])
            def _():
                pl.semaphore_signal(
                    ready.at[d - 1], inc=1, device_id=seq_dev(-d), device_id_type=MESH
                )

    def remote(src, dst, s_sem, r_sem, dev):
        return pltpu.make_async_remote_copy(
            src_ref=src, dst_ref=dst, send_sem=s_sem, recv_sem=r_sem,
            device_id=dev, device_id_type=MESH,
        )

    def send(src, dst, s_sem, r_sem, dev):
        copy = remote(src, dst, s_sem, r_sem, dev)
        copy.start()
        return copy

    pair = [send(d_mine, d_part, sa_sem.at[0], ra_sem.at[0], partner)]
    for copy in x_in:
        copy.wait()
    other = 1 - core
    for k in range(nh):
        half = other if k < 2 else core
        j = k % 2
        h = half * 2 + j
        lhs = bt[...] * wdev[pl.ds(h, 1), :].astype(BF16)
        s_mine[h] = mm(lhs, x_s[half, :, j * 128 : (j + 1) * 128])
        pair.append(send(s_mine.at[h], s_part.at[h], sa_sem.at[1 + k], ra_sem.at[1 + k], partner))

    for copy in c_in:
        copy.wait()
    for c in range(nc):
        part = mm(pick, c_s[c * 16 : (c + 1) * 16].reshape(2 * L, 128))
        csel[c * L : (c + 1) * L, :] = part.astype(BF16)

    is_second = core == 1
    mine = [core * 2 + j for j in range(2)]
    pair[0].wait_recv()
    ring, far, chip_d = ([], [], [])
    if chain:
        for j in range(2):
            chip_d.append(d_mine[mine[j]][0:1] * d_part[mine[j]][0:1])
            dc_send[j] = jnp.broadcast_to(chip_d[j], (8, L))
        ring = [remote(dc_send, dq1, sa_sem.at[5], ra_sem.at[5], seq_dev(1))]
        for j in range(2):
            ring.append(
                remote(c_send.at[j], q1.at[j], sa_sem.at[6 + j], ra_sem.at[6 + j], seq_dev(1))
            )
            far.append(
                remote(t_send.at[j], q2.at[j], sa_sem.at[8 + j], ra_sem.at[8 + j], seq_dev(2))
            )

        late = z == 2
        early = feeds[1] & jnp.logical_not(late)

        @pl.when(early)
        def _():
            pl.semaphore_wait(ready.at[0], 1)
            ring[0].start()

        for j in range(2):
            pair[1 + j].wait_recv()
            sm, sp = (s_mine[mine[j]], s_part[mine[j]])
            earlier = jnp.where(is_second, sp, sm)
            latter = jnp.where(is_second, sm, sp)
            d_latter = jnp.where(is_second, d_mine[mine[j]][0:1], d_part[mine[j]][0:1])
            chip_s = d_latter * earlier + latter
            h_mine[j] = chip_s
            c_send[j] = chip_s.astype(BF16)

            @pl.when(early)
            def _():
                ring[1 + j].start()

        @pl.when(z == 0)
        def _():
            pl.semaphore_wait(ready.at[1], 1)
            for j in range(2):
                t_send[j] = c_send[j]
                far[j].start()

    else:
        for j in range(2):
            pair[1 + j].wait_recv()

    state[...] = jnp.zeros_like(state)
    lower = ki >= kj

    def chunk(c):
        at = pl.multiple_of(c * L, L)
        col = colb[pl.ds(at, L), :]
        row = rows[c]
        cc = csel[pl.ds(at, L), :]
        gram = nt(cc, bsel[pl.ds(at, L), :])
        same = col[:, 12:13] == row[16:17]
        gram = jnp.where(same & lower, gram, 0.0)
        cf = cc.astype(F32)
        btc = bt[:, pl.ds(at, L)]
        for h in range(nh):
            half, hs = (h // 2, slice(h % 2 * 128, (h % 2 + 1) * 128))
            gap = jnp.minimum(col[:, h : h + 1] - row[h : h + 1], 0.0)
            w = (gram * jnp.exp(gap) * row[nh + h : nh + h + 1]).astype(BF16)
            xh = x_s[half, pl.ds(at, L), hs]
            st = state[h]
            cw = (cf * col[:, nh + h : nh + h + 1]).astype(BF16)
            y = mm(w, xh) + mm(cw, st.astype(BF16)) + d_skip[h] * xh.astype(F32)
            ypre[half, pl.ds(at, L), hs] = y
            new = btc * row[2 * nh + h : 2 * nh + h + 1].astype(BF16)
            state[h] = st * row[3 * nh + h : 3 * nh + h + 1] + mm(new, xh)

    def chunks(i, carry_in):
        chunk(2 * i)
        chunk(2 * i + 1)
        return carry_in

    def silu(c, carry_in):
        at = pl.multiple_of(c * L, L)
        for half in range(2):
            v = z_s[half, pl.ds(at, L), :].astype(F32)
            sz[half, pl.ds(at, L), :] = v / (1.0 + jnp.exp(-v))
        return carry_in

    cut = nc // 4
    lax.fori_loop(0, cut, chunks, 0)

    if chain:

        @pl.when(late)
        def _():
            pl.semaphore_wait(ready.at[0], 1)
            for copy in ring:
                copy.start()

        @pl.when(has[1])
        def _():
            ring[0].wait_recv()
            for j in range(2):
                ring[1 + j].wait_recv()
                t_send[j] = (h_mine[j] + chip_d[j] * q1[j].astype(F32)).astype(BF16)
                if j == 0:

                    @pl.when(feeds[2])
                    def _():
                        pl.semaphore_wait(ready.at[1], 1)

                @pl.when(feeds[2])
                def _():
                    far[j].start()

    for copy in z_in:
        copy.wait()
    lax.fori_loop(cut, nc // 2, chunks, 0)
    lax.fori_loop(0, nc, silu, 0)
    for copy in a_in:
        copy.wait()
    pair[3].wait_recv()
    pair[4].wait_recv()
    for copy in pair:
        copy.wait_send()
    if chain:

        @pl.when(feeds[1])
        def _():
            for copy in ring:
                copy.wait_send()


    def entering(inc, h):
        second = d_part[h][0:1] * inc + s_part[h]
        return jnp.where(is_second, second, inc).astype(BF16)

    back = []
    for j in range(2):
        js = slice(j * 128, (j + 1) * 128)
        if chain:

            @pl.when(z == 0)
            def _():
                h_send[j] = jnp.zeros((128, 128), F32)

            @pl.when(z == 1)
            def _():
                h_send[j] = q1[j].astype(F32)

            @pl.when(has[2])
            def _():
                far[j].wait_recv()
                h_send[j] = q1[j].astype(F32) + dq1[j][0:1] * q2[j].astype(F32)

            inc = h_send[j]
            back.append(
                send(h_send.at[j], h_part.at[j], sa_sem.at[10 + j], ra_sem.at[10 + j], partner)
            )
        else:
            inc = jnp.zeros((128, 128), F32)
        hb[core, :, js] = entering(inc, mine[j])

    one8 = jnp.ones((8, L), BF16)

    def gate(q, half, last):
        at = q * qt if isinstance(q, int) else pl.multiple_of(q * qt, qt)
        here = pl.ds(at, qt)
        col = colb[here, :]
        cc = csel[here, :]
        sq = sqs[here, :] if last else None
        picked = pick_s[here, :] if last else None
        for j in range(2):
            js = slice(j * 128, (j + 1) * 128)
            lo = col[:, 2 * nh + j : 2 * nh + j + 1]
            hi = col[:, 2 * nh + 2 + j : 2 * nh + 3 + j]
            ent = mm(cc, hb[half, :, js]) * jnp.where(half == 1, hi, lo)
            gated = (ypre[half, here, js] + ent) * sz[half, here, js]
            sq = gated * gated if sq is None else sq + gated * gated
            g_s[half, here, js] = (gated * gain_s[half, 0:1, js]).astype(BF16)
        lg = col[:, 13:14]
        for k in range(0, 4, 2):
            two = mm(g_s[half, here, :], a_s[half, :, k * 128 : (k + 2) * 128])
            for j in range(2):
                one = jnp.where(lg == float(k + j), two[:, j * 128 : (j + 1) * 128], 0.0)
                picked = one if picked is None else picked + one
        if last:
            sums = nt(one8, sq.astype(BF16))
            for i in range(qt // L):
                ss_mine[pl.ds(q * (qt // L) + i, 1), :] = sums[0:1, i * L : (i + 1) * L]
            pbuf[q] = picked.astype(BF16)
        else:
            sqs[here, :] = sq
            pick_s[here, :] = picked

    for q in range(xn):
        gate(q, core, False)
    for j in range(2):
        if chain:
            back[j].wait_recv()
            inc = h_part[j]
        else:
            inc = jnp.zeros((128, 128), F32)
        hb[other, :, j * 128 : (j + 1) * 128] = entering(inc, other * 2 + j)
    for copy in back:
        copy.wait_send()
    if chain:

        @pl.when(feeds[2])
        def _():
            for copy in far:
                copy.wait_send()

    sends = []
    order = sorted(range(1, xn), key=lambda i: -min(i, xn - i))
    for i in order:
        q = lax.rem(mx + i, xn)
        gate(q, other, True)
        sends.append(send(pbuf.at[q], rx.at[mx], sx_sem.at[i], rx_sem.at[mx], x_dev(i)))
    gate(mx, other, True)
    for i in order:
        sends.append(send(ss_mine, ss_rx.at[mx], ssx_s.at[i], ssx_r.at[mx], x_dev(i)))

    def arrived(dst, sem):
        pltpu.make_async_remote_copy(
            src_ref=dst, dst_ref=dst, send_sem=in_sem.at[0], recv_sem=sem,
            device_id=partner, device_id_type=MESH,
        ).wait_recv()

    total = pbuf[mx].astype(F32)
    for i in order[::-1]:
        src = lax.rem(mx + i, xn)
        arrived(rx.at[src], rx_sem.at[src])
        total = total + rx[src].astype(F32)
    qsum[...] = total.astype(BF16).reshape(qsum.shape)
    y_order = sorted(range(1, yn), key=lambda i: -min(i, yn - i))
    for i in y_order:
        p = lax.rem(my + i, yn)
        sends.append(send(qsum.at[p], ry.at[my], sy_sem.at[i], ry_sem.at[my], y_dev(i)))
    ss = ss_mine[...]
    for i in order[::-1]:
        src = lax.rem(mx + i, xn)
        arrived(ss_rx.at[src], ssx_r.at[src])
        ss = ss + ss_rx[src]
    ss_x[...] = ss
    for i in y_order:
        sends.append(send(ss_x, ss_ry.at[my], ssy_s.at[i], ssy_r.at[my], y_dev(i)))
    piece = qsum[my].astype(F32)
    for i in y_order[::-1]:
        src = lax.rem(my + i, yn)
        arrived(ry.at[src], ry_sem.at[src])
        piece = piece + ry[src].astype(F32)
    lbuf[mx, my] = piece.astype(BF16)
    for i in y_order:
        sends.append(send(lbuf.at[mx, my], lbuf.at[mx, my], sgy_sem.at[i], rgy_sem.at[my], y_dev(i)))

    def forward(p, k):
        for i in order:
            sends.append(
                send(lbuf.at[mx, p], lbuf.at[mx, p], sgx_sem.at[i, k], rgx_sem.at[mx], x_dev(i))
            )

    forward(my, 0)

    for i in y_order[::-1]:
        src = lax.rem(my + i, yn)
        arrived(ss_ry.at[src], ssy_r.at[src])
        ss = ss + ss_ry[src]
    scale = lax.rsqrt(ss / (SPACE_HEADS * HEAD_DIM) + 1e-05)
    eye = ki == kj
    for c in range(nc):
        spread = jnp.broadcast_to(scale[c : c + 1], (L, L))
        one = jnp.sum(jnp.where(eye, spread, 0.0), axis=1, keepdims=True)
        colscale[c * L : (c + 1) * L, :] = jnp.broadcast_to(one, (L, L))

    for i in y_order[::-1]:
        p = lax.rem(my + i, yn)
        arrived(lbuf.at[mx, p], rgy_sem.at[p])
        forward(p, i)

    u_in.wait()

    def finish(q):
        at = pl.multiple_of(q * qt, qt)
        here = pl.ds(at, qt)
        lg = colb[here, 13:14]
        low = lbuf[q].reshape(qt, 128)
        sel = jnp.concatenate(
            [jnp.where(lg == float(k), low, jnp.zeros_like(low)) for k in range(4)], axis=1
        )
        scl = colscale[here, :]
        for h in range(0, nh, 2):
            lift = mm(sel, u_s[:, h * 128 : (h + 2) * 128])
            for j in range(2):
                hs = slice((h + j) * 128, (h + j + 1) * 128)
                val = g_s[h // 2, here, j * 128 : (j + 1) * 128].astype(F32) + lift[:, j * 128 : (j + 1) * 128]
                out_s[here, hs] = (val * scl).astype(BF16)
        copy = pltpu.make_async_copy(
            out_s.at[here, :], out_hbm.at[here, :], out_sem.at[q]
        )
        copy.start()
        return copy

    outs = [finish(mx)]
    for i in order[::-1]:
        q = lax.rem(mx + i, xn)
        arrived(lbuf.at[q], rgx_sem.at[q])
        outs.append(finish(q))
    for copy in sends:
        copy.wait_send()
    for copy in outs:
        copy.wait()


def per_device(seq_n, xn, yn, x_in, z_gate, b_input, c_input, dt_raw, a_log, d_skip, norm_gain,
               doc_lengths, doc_lang, adapt_down, adapt_up):
    tok, feat = x_in.shape
    nh = dt_raw.shape[0]
    nc = tok // L
    qt = tok // xn
    pt = qt // yn
    half = feat // 2
    dma = pltpu.SemaphoreType.DMA
    vm = pltpu.VMEM
    scratch = [
        pltpu.SMEM(doc_lengths.shape, jnp.int32),
        pltpu.SMEM(doc_lang.shape, jnp.int32),
        pltpu.SMEM((nh,), F32),
        pltpu.SMEM((nh,), F32),
        vm((nh, tok), F32),
        vm((1, feat), F32),
        vm((2, 8, half), F32),
        vm((2, tok, half), BF16),
        vm((2, tok, half), BF16),
        vm((tok // 8, 16, 128), BF16),
        vm((tok // 8, 16, 128), BF16),
        vm((2, half, 512), BF16),
        vm((512, feat), BF16),
        vm((2, tok, half), F32),
        vm((2, tok, half), F32),
        vm((2, tok, half), BF16),
        vm((tok, feat), BF16),
        vm((tok, L), F32),
        vm((tok, L), F32),
        vm((nc * nh, L), F32),
        vm((nc, 16, L), F32),
        vm((nc, 24, L), F32),
        vm((nh, tok), F32),
        vm((tok, L), F32),
        vm((tok, L), BF16),
        vm((tok, L), BF16),
        vm((L, tok), BF16),
        vm((nh, 128, 128), F32),
        vm((nh, 128, 128), F32),
        vm((nh, 128, 128), F32),
        vm((nh, 8, L), F32),
        vm((nh, 8, L), F32),
        vm((2, 128, 128), BF16),
        vm((2, 128, 128), BF16),
        vm((2, 8, L), F32),
        vm((2, 8, L), F32),
        vm((2, 128, 128), BF16),
        vm((2, 128, 128), BF16),
        vm((2, 128, 128), F32),
        vm((2, 128, 128), F32),
        vm((2, 128, 128), F32),
        vm((2, 128, half), BF16),
        vm((xn, qt, 128), BF16),
        vm((xn, qt, 128), BF16),
        vm((yn, pt, 128), BF16),
        vm((yn, pt, 128), BF16),
        vm((xn, yn, pt, 128), BF16),
        vm((nc, L), F32),
        vm((xn, nc, L), F32),
        vm((nc, L), F32),
        vm((yn, nc, L), F32),
        vm((tok, L), F32),
        dma((39,)),
        dma((xn,)),
        dma((12,)),
        dma((12,)),
        dma((xn,)),
        dma((xn,)),
        dma((yn,)),
        dma((yn,)),
        dma((yn,)),
        dma((yn,)),
        dma((xn, yn)),
        dma((xn,)),
        dma((xn,)),
        dma((xn,)),
        dma((yn,)),
        dma((yn,)),
        pltpu.SemaphoreType.REGULAR((2,)),
    ]
    hbm = pl.BlockSpec(memory_space=pltpu.HBM)
    call = pl.pallas_call(
        functools.partial(kernel_body, seq_n, xn, yn),
        out_shape=jax.ShapeDtypeStruct((tok, feat), BF16),
        in_specs=[hbm] * 12,
        out_specs=pl.BlockSpec(memory_space=pl.ANY),
        scratch_shapes=scratch,
        compiler_params=pltpu.CompilerParams(
            collective_id=0, has_side_effects=True, vmem_limit_bytes=40 * 1024 * 1024
        ),
    )
    operands = (
        doc_lengths,
        doc_lang,
        a_log,
        d_skip,
        dt_raw,
        norm_gain.reshape(1, feat),
        x_in,
        z_gate,
        b_input.reshape(tok // 8, 8, GROUPS // 2, 2, 128),
        c_input.reshape(tok // 8, 8, GROUPS // 2, 2, 128),
        adapt_down,
        adapt_up.reshape(512, feat),
    )
    return call(*[pltpu.with_memory_space_constraint(v, pltpu.HBM) for v in operands])


def solution(mesh):
    seq_n, head_n = mesh.shape["seq"], mesh.shape["head"]
    xn = 4 if head_n == 32 else min(2, head_n)
    placed = (
        P("seq", "head"),
        P("seq", "head"),
        P("seq", None, None),
        P("seq", None, None),
        P("head", "seq"),
        P("head"),
        P("head"),
        P("head"),
        P(),
        P(),
        P(None, "head", None),
        P(None, None, "head"),
    )
    return jax.shard_map(
        functools.partial(per_device, seq_n, xn, head_n // xn),
        mesh=mesh, in_specs=placed, out_specs=P("seq", "head"), check_vma=False,
    )
```

```python
import functools

import jax
import jax.numpy as jnp
from jax import lax
from jax.experimental import pallas as pl
from jax.experimental.pallas import tpu as pltpu
from jax.sharding import PartitionSpec as P

SPACE_HEADS = 128
HEAD_DIM = 128
GROUPS = 8
L = 128
MESH = pl.DeviceIdType.MESH
F32 = jnp.float32
BF16 = jnp.bfloat16
HIGHEST = lax.Precision.HIGHEST


def nt(a, b, precision=None):
    return lax.dot_general(
        a, b, (((1,), (1,)), ((), ())), preferred_element_type=F32, precision=precision
    )


def mm(a, b, precision=None):
    return jnp.dot(a, b, preferred_element_type=F32, precision=precision)


def kernel_body(
    seq_n,
    xn,
    yn,
    doc_len_hbm,
    doc_lang_hbm,
    a_log_hbm,
    d_skip_hbm,
    dt_hbm,
    gain_hbm,
    x_hbm,
    z_hbm,
    b_hbm,
    c_hbm,
    down_hbm,
    up_hbm,
    out_ref,
    doc_len,
    doc_lang,
    a_log,
    d_skip,
    dt_ref,
    gain_ref,
    gain_s,
    x_s,
    z_s,
    b_s,
    c_s,
    a_s,
    u_s,
    ypre,
    sz,
    g_s,
    sqs,
    pick_s,
    dt32,
    rowb,
    rows,
    wdev,
    colb,
    csel,
    bsel,
    bt,
    state,
    s_mine,
    s_part,
    d_mine,
    d_part,
    c_send,
    q1,
    dc_send,
    dq1,
    t_send,
    q2,
    h_mine,
    h_send,
    h_part,
    hb,
    pbuf,
    rx,
    qsum,
    ry,
    lbuf,
    ss_mine,
    ss_rx,
    ss_x,
    ss_ry,
    colscale,
    in_sem,
    sa_sem,
    ra_sem,
    sx_sem,
    rx_sem,
    sy_sem,
    ry_sem,
    sgy_sem,
    rgy_sem,
    sgx_sem,
    rgx_sem,
    ssx_s,
    ssx_r,
    ssy_s,
    ssy_r,
    ready,
):
    tok = x_s.shape[1]
    nc = tok // L
    nh = dt_ref.shape[0]
    qt = tok // xn
    pt = qt // yn
    rank = lax.axis_index("seq")
    hd = lax.axis_index("head")
    core = lax.rem(rank, 2)
    z = rank // 2
    nz = seq_n // 2
    mx = hd // yn
    my = lax.rem(hd, yn)
    group = hd * nh // (SPACE_HEADS // GROUPS)

    def seq_dev(dz):
        return (lax.rem(z + dz + nz, nz) * 2 + core, hd)

    partner = (z * 2 + 1 - core, hd)

    def x_dev(i):
        return (rank, lax.rem(mx + i, xn) * yn + my)

    def y_dev(i):
        return (rank, mx * yn + lax.rem(my + i, yn))

    chain = nz > 4
    has = {1: z >= 1, 2: z >= 2}
    feeds = {1: z < nz - 1, 2: z < nz - 2}
    peers = [partner]
    peers += [x_dev(i) for i in range(1, xn)]
    peers += [y_dev(i) for i in range(1, yn)]
    def load(src, dst, k):
        copy = pltpu.make_async_copy(src, dst, in_sem.at[k])
        copy.start()
        return copy

    small = [
        load(src, dst, 9 + k)
        for k, (src, dst) in enumerate(
            (
                (dt_hbm, dt_ref),
                (a_log_hbm, a_log),
                (doc_len_hbm, doc_len),
                (doc_lang_hbm, doc_lang),
                (d_skip_hbm, d_skip),
                (gain_hbm, gain_ref),
            )
        )
    ]
    def load_pair(src, dst, k):
        return [
            load(src.at[:, j, group // 2], dst.at[:, 2 * j : 2 * j + 2, :], k + j)
            for j in range(8)
        ]

    b_in = load_pair(b_hbm, b_s, 15)
    barrier = pltpu.get_barrier_semaphore()
    for peer in peers:
        pl.semaphore_signal(barrier, inc=1, device_id=peer, device_id_type=MESH)
    if chain:
        for d in (1, 2):

            @pl.when(feeds[d])
            def _():
                pl.semaphore_signal(barrier, inc=1, device_id=seq_dev(d), device_id_type=MESH)

    x_in = [load(x_hbm.at[:, pl.ds(k * 256, 256)], x_s.at[k], k) for k in range(2)]

    for copy in small:
        copy.wait()
    for c in range(nc):
        dt32[pl.ds(c * nh, nh), :] = dt_ref[:, pl.ds(c * L, L)]
    shape = (nc * nh, L)
    rid = lax.broadcasted_iota(jnp.int32, shape, 0)
    lane = lax.broadcasted_iota(jnp.int32, shape, 1)
    head_of = rid & (nh - 1)
    chunk_of = lax.shift_right_logical(rid, nh.bit_length() - 1)
    raw = dt32[...]
    dt = jnp.maximum(raw, 0.0) + jnp.log1p(jnp.exp(-jnp.abs(raw)))
    alog = jnp.full(shape, a_log[0], F32)
    for h in range(1, nh):
        alog = jnp.where(head_of == h, a_log[h], alog)
    ld = dt * -jnp.exp(alog)
    ki = lax.broadcasted_iota(jnp.int32, (L, L), 0)
    kj = lax.broadcasted_iota(jnp.int32, (L, L), 1)
    cum = mm(ld, (ki <= kj).astype(F32), HIGHEST)
    suf = mm(ld, (ki > kj).astype(F32), HIGHEST)
    tot = jnp.broadcast_to(jnp.sum(ld, axis=1, keepdims=True), shape)

    def down(v, k):
        return jnp.where(rid >= k, pltpu.roll(v, k, 0), 0.0)

    def up(v, k):
        return jnp.where(rid < nc * nh - k, pltpu.roll(v, nc * nh - k, 0), 0.0)

    pre, post = (down(tot, nh), up(tot, nh))
    step = nh
    while step < nc * nh:
        pre = pre + down(pre, step)
        post = post + up(post, step)
        step *= 2
    starts, first = ([], jnp.int32(0))
    for k in range(doc_len.shape[0]):
        starts.append(first)
        first = first + doc_len[k]
    base = rank * tok

    def docs(t):
        total = None
        for s in starts:
            one = (t >= s).astype(jnp.int32)
            total = one if total is None else total + one
        return total

    n_t = docs(base + chunk_of * L + lane)
    n_cs = docs(base + chunk_of * L - 1)
    n_ce = docs(base + chunk_of * L + (L - 1))
    n_bs = docs(base + 0 * chunk_of - 1)
    n_be = docs(base + 0 * chunk_of + (tok - 1))
    lang = jnp.zeros(shape, jnp.int32)
    for k in range(doc_lang.shape[0]):
        lang = jnp.where(n_t == k + 1, doc_lang[k], lang)

    def keep(cond, v):
        return jnp.where(cond, v, 0.0)

    carry = keep(n_t == n_cs, jnp.exp(cum))
    enter = keep(n_t == n_bs, jnp.exp(pre + cum))
    w_dev = keep(n_t == n_be, jnp.exp(suf + post)) * dt
    w_chunk = keep(n_t == n_ce, jnp.exp(suf)) * dt
    kept = keep(n_ce == n_cs, jnp.exp(tot))
    through = keep(n_be == n_bs, jnp.exp(pre + tot))
    n_f = n_t.astype(F32)
    lang_f = lang.astype(F32)
    for c in range(nc):
        own = slice(c * nh, (c + 1) * nh)
        for k, v in enumerate((cum, carry, enter)):
            rowb[c, k * nh : (k + 1) * nh, :] = v[own]
        rowb[c, 12:13, :] = n_f[c * nh : c * nh + 1]
        rowb[c, 13:14, :] = lang_f[c * nh : c * nh + 1]
        rowb[c, 14:16, :] = jnp.zeros((2, L), F32)
        for k, v in enumerate((cum, dt, w_chunk, kept)):
            rows[c, k * nh : (k + 1) * nh, :] = v[own]
        rows[c, 16:17, :] = n_f[c * nh : c * nh + 1]
        wdev[:, c * L : (c + 1) * L] = w_dev[own]
    for h in range(nh):
        r = (nc - 1) * nh + h
        d_mine[h] = jnp.broadcast_to(through[r : r + 1], (8, L))
    for k in range(2):
        gain_s[k] = jnp.broadcast_to(gain_ref[0:1, k * 256 : (k + 1) * 256], (8, 256))
    cols = jnp.transpose(rowb[...].reshape(nc * 16, L))
    for c in range(nc):
        colb[c * L : (c + 1) * L, 0:16] = cols[:, c * 16 : (c + 1) * 16]

    pr = lax.broadcasted_iota(jnp.int32, (L, L * 2), 0)
    pc = lax.broadcasted_iota(jnp.int32, (L, L * 2), 1)
    pick = (pc == pr * 2 + lax.rem(group, 2)).astype(BF16)
    for copy in b_in:
        copy.wait()
    c_in = load_pair(c_hbm, c_s, 23)
    z_in = [load(z_hbm.at[:, pl.ds(k * 256, 256)], z_s.at[k], 2 + k) for k in range(2)]
    a_in = [
        load(
            down_hbm.at[k % 4, pl.ds(k // 4 * 256, 256), :],
            a_s.at[k // 4, :, pl.ds(k % 4 * 128, 128)],
            31 + k,
        )
        for k in range(8)
    ]
    u_in = load(up_hbm, u_s, 8)
    for c in range(nc):
        part = mm(pick, b_s[c * 16 : (c + 1) * 16].reshape(2 * L, 128)).astype(BF16)
        bsel[c * L : (c + 1) * L, :] = part
        bt[:, c * L : (c + 1) * L] = jnp.transpose(part)
    pl.semaphore_wait(barrier, len(peers) + (jnp.minimum(z, 2) if chain else 0))
    if chain:
        for d in (1, 2):

            @pl.when(has[d])
            def _():
                pl.semaphore_signal(
                    ready.at[d - 1], inc=1, device_id=seq_dev(-d), device_id_type=MESH
                )

    def remote(src, dst, s_sem, r_sem, dev):
        return pltpu.make_async_remote_copy(
            src_ref=src, dst_ref=dst, send_sem=s_sem, recv_sem=r_sem,
            device_id=dev, device_id_type=MESH,
        )

    def send(src, dst, s_sem, r_sem, dev):
        copy = remote(src, dst, s_sem, r_sem, dev)
        copy.start()
        return copy

    pair = [send(d_mine, d_part, sa_sem.at[0], ra_sem.at[0], partner)]
    for copy in x_in:
        copy.wait()
    other = 1 - core
    for k in range(nh):
        half = other if k < 2 else core
        j = k % 2
        h = half * 2 + j
        lhs = bt[...] * wdev[pl.ds(h, 1), :].astype(BF16)
        s_mine[h] = mm(lhs, x_s[half, :, j * 128 : (j + 1) * 128])
        pair.append(send(s_mine.at[h], s_part.at[h], sa_sem.at[1 + k], ra_sem.at[1 + k], partner))

    for copy in c_in:
        copy.wait()
    for c in range(nc):
        part = mm(pick, c_s[c * 16 : (c + 1) * 16].reshape(2 * L, 128))
        csel[c * L : (c + 1) * L, :] = part.astype(BF16)

    is_second = core == 1
    state[...] = jnp.zeros_like(state)
    lower = ki >= kj

    def chunk(c):
        at = pl.multiple_of(c * L, L)
        col = colb[pl.ds(at, L), :]
        row = rows[c]
        cc = csel[pl.ds(at, L), :]
        gram = nt(cc, bsel[pl.ds(at, L), :])
        same = col[:, 12:13] == row[16:17]
        gram = jnp.where(same & lower, gram, 0.0)
        cf = cc.astype(F32)
        btc = bt[:, pl.ds(at, L)]
        for h in range(nh):
            half, hs = (h // 2, slice(h % 2 * 128, (h % 2 + 1) * 128))
            gap = jnp.minimum(col[:, h : h + 1] - row[h : h + 1], 0.0)
            w = (gram * jnp.exp(gap) * row[nh + h : nh + h + 1]).astype(BF16)
            xh = x_s[half, pl.ds(at, L), hs]
            st = state[h]
            cw = (cf * col[:, nh + h : nh + h + 1]).astype(BF16)
            y = mm(w, xh) + mm(cw, st.astype(BF16)) + d_skip[h] * xh.astype(F32)
            ypre[half, pl.ds(at, L), hs] = y
            new = btc * row[2 * nh + h : 2 * nh + h + 1].astype(BF16)
            state[h] = st * row[3 * nh + h : 3 * nh + h + 1] + mm(new, xh)

    def chunks(i, carry_in):
        chunk(2 * i)
        chunk(2 * i + 1)
        return carry_in

    def silu(c, carry_in):
        at = pl.multiple_of(c * L, L)
        for half in range(2):
            v = z_s[half, pl.ds(at, L), :].astype(F32)
            sz[half, pl.ds(at, L), :] = v / (1.0 + jnp.exp(-v))
        return carry_in

    cut = nc // 4

    @pl.when(core == 0)
    def _():
        lax.fori_loop(0, cut, chunks, 0)

    mine = [core * 2 + j for j in range(2)]
    pair[0].wait_recv()
    ring, far, chip_d = ([], [], [])
    if chain:
        for j in range(2):
            chip_d.append(d_mine[mine[j]][0:1] * d_part[mine[j]][0:1])
            dc_send[j] = jnp.broadcast_to(chip_d[j], (8, L))
        ring = [remote(dc_send, dq1, sa_sem.at[5], ra_sem.at[5], seq_dev(1))]
        for j in range(2):
            ring.append(
                remote(c_send.at[j], q1.at[j], sa_sem.at[6 + j], ra_sem.at[6 + j], seq_dev(1))
            )
            far.append(
                remote(t_send.at[j], q2.at[j], sa_sem.at[8 + j], ra_sem.at[8 + j], seq_dev(2))
            )

        late = z == 2
        early = feeds[1] & jnp.logical_not(late)

        for j in range(2):
            pair[1 + j].wait_recv()
            sm, sp = (s_mine[mine[j]], s_part[mine[j]])
            earlier = jnp.where(is_second, sp, sm)
            latter = jnp.where(is_second, sm, sp)
            d_latter = jnp.where(is_second, d_mine[mine[j]][0:1], d_part[mine[j]][0:1])
            chip_s = d_latter * earlier + latter
            h_mine[j] = chip_s
            c_send[j] = chip_s.astype(BF16)


        @pl.when(z == 0)
        def _():
            for j in range(2):
                t_send[j] = c_send[j]

    else:
        for j in range(2):
            pair[1 + j].wait_recv()

    @pl.when(is_second)
    def _():
        lax.fori_loop(0, 1, chunks, 0)

    if chain:

        @pl.when(early)
        def _():
            pl.semaphore_wait(ready.at[0], 1)
            for copy in ring:
                copy.start()

        @pl.when(z == 0)
        def _():
            pl.semaphore_wait(ready.at[1], 1)
            for copy in far:
                copy.start()

    @pl.when(is_second)
    def _():
        lax.fori_loop(1, cut, chunks, 0)


    if chain:

        @pl.when(late)
        def _():
            pl.semaphore_wait(ready.at[0], 1)
            for copy in ring:
                copy.start()

        @pl.when(has[1])
        def _():
            ring[0].wait_recv()
            for j in range(2):
                ring[1 + j].wait_recv()
                t_send[j] = (h_mine[j] + chip_d[j] * q1[j].astype(F32)).astype(BF16)
                if j == 0:

                    @pl.when(feeds[2])
                    def _():
                        pl.semaphore_wait(ready.at[1], 1)

                @pl.when(feeds[2])
                def _():
                    far[j].start()

    for copy in z_in:
        copy.wait()
    lax.fori_loop(cut, nc // 2, chunks, 0)
    lax.fori_loop(0, nc, silu, 0)
    for copy in a_in:
        copy.wait()
    pair[3].wait_recv()
    pair[4].wait_recv()
    def entering(inc, h):
        second = d_part[h][0:1] * inc + s_part[h]
        return jnp.where(is_second, second, inc).astype(BF16)

    back = []
    for j in range(2):
        js = slice(j * 128, (j + 1) * 128)
        if chain:

            @pl.when(z == 0)
            def _():
                h_send[j] = jnp.zeros((128, 128), F32)

            @pl.when(z == 1)
            def _():
                h_send[j] = q1[j].astype(F32)

            @pl.when(has[2])
            def _():
                far[j].wait_recv()
                h_send[j] = q1[j].astype(F32) + dq1[j][0:1] * q2[j].astype(F32)

            inc = h_send[j]
            back.append(
                send(h_send.at[j], h_part.at[j], sa_sem.at[10 + j], ra_sem.at[10 + j], partner)
            )
        else:
            inc = jnp.zeros((128, 128), F32)
        hb[core, :, js] = entering(inc, mine[j])

    one8 = jnp.ones((8, L), BF16)

    def gate(q, half, last):
        at = q * qt if isinstance(q, int) else pl.multiple_of(q * qt, qt)
        here = pl.ds(at, qt)
        col = colb[here, :]
        cc = csel[here, :]
        sq = sqs[here, :] if last else None
        picked = pick_s[here, :] if last else None
        for j in range(2):
            js = slice(j * 128, (j + 1) * 128)
            lo = col[:, 2 * nh + j : 2 * nh + j + 1]
            hi = col[:, 2 * nh + 2 + j : 2 * nh + 3 + j]
            ent = mm(cc, hb[half, :, js]) * jnp.where(half == 1, hi, lo)
            gated = (ypre[half, here, js] + ent) * sz[half, here, js]
            sq = gated * gated if sq is None else sq + gated * gated
            g_s[half, here, js] = (gated * gain_s[half, 0:1, js]).astype(BF16)
        lg = col[:, 13:14]
        for k in range(0, 4, 2):
            two = mm(g_s[half, here, :], a_s[half, :, k * 128 : (k + 2) * 128])
            for j in range(2):
                one = jnp.where(lg == float(k + j), two[:, j * 128 : (j + 1) * 128], 0.0)
                picked = one if picked is None else picked + one
        if last:
            sums = nt(one8, sq.astype(BF16))
            for i in range(qt // L):
                ss_mine[pl.ds(q * (qt // L) + i, 1), :] = sums[0:1, i * L : (i + 1) * L]
            pbuf[q] = picked.astype(BF16)
        else:
            sqs[here, :] = sq
            pick_s[here, :] = picked

    for q in range(xn):
        gate(q, core, False)
    for j in range(2):
        if chain:
            back[j].wait_recv()
            inc = h_part[j]
        else:
            inc = jnp.zeros((128, 128), F32)
        hb[other, :, j * 128 : (j + 1) * 128] = entering(inc, other * 2 + j)
    sends = []
    order = sorted(range(1, xn), key=lambda i: -min(i, xn - i))
    for i in order:
        q = lax.rem(mx + i, xn)
        gate(q, other, True)
        sends.append(send(pbuf.at[q], rx.at[mx], sx_sem.at[i], rx_sem.at[mx], x_dev(i)))
    gate(mx, other, True)
    for i in order:
        sends.append(send(ss_mine, ss_rx.at[mx], ssx_s.at[i], ssx_r.at[mx], x_dev(i)))

    def arrived(dst, sem):
        pltpu.make_async_remote_copy(
            src_ref=dst, dst_ref=dst, send_sem=in_sem.at[0], recv_sem=sem,
            device_id=partner, device_id_type=MESH,
        ).wait_recv()

    total = pbuf[mx].astype(F32)
    for i in order[::-1]:
        src = lax.rem(mx + i, xn)
        arrived(rx.at[src], rx_sem.at[src])
        total = total + rx[src].astype(F32)
    qsum[...] = total.astype(BF16).reshape(qsum.shape)
    y_order = sorted(range(1, yn), key=lambda i: -min(i, yn - i))
    for i in y_order:
        p = lax.rem(my + i, yn)
        sends.append(send(qsum.at[p], ry.at[my], sy_sem.at[i], ry_sem.at[my], y_dev(i)))
    ss = ss_mine[...]
    for i in order[::-1]:
        src = lax.rem(mx + i, xn)
        arrived(ss_rx.at[src], ssx_r.at[src])
        ss = ss + ss_rx[src]
    ss_x[...] = ss
    for i in y_order:
        sends.append(send(ss_x, ss_ry.at[my], ssy_s.at[i], ssy_r.at[my], y_dev(i)))
    piece = qsum[my].astype(F32)
    for i in y_order[::-1]:
        src = lax.rem(my + i, yn)
        arrived(ry.at[src], ry_sem.at[src])
        piece = piece + ry[src].astype(F32)
    lbuf[mx, my] = piece.astype(BF16)
    for i in y_order:
        sends.append(send(lbuf.at[mx, my], lbuf.at[mx, my], sgy_sem.at[i], rgy_sem.at[my], y_dev(i)))

    def forward(p, k):
        for i in order:
            sends.append(
                send(lbuf.at[mx, p], lbuf.at[mx, p], sgx_sem.at[i, k], rgx_sem.at[mx], x_dev(i))
            )

    forward(my, 0)

    for i in y_order[::-1]:
        src = lax.rem(my + i, yn)
        arrived(ss_ry.at[src], ssy_r.at[src])
        ss = ss + ss_ry[src]
    scale = lax.rsqrt(ss / (SPACE_HEADS * HEAD_DIM) + 1e-05)
    eye = ki == kj
    for c in range(nc):
        spread = jnp.broadcast_to(scale[c : c + 1], (L, L))
        one = jnp.sum(jnp.where(eye, spread, 0.0), axis=1, keepdims=True)
        colscale[c * L : (c + 1) * L, :] = jnp.broadcast_to(one, (L, L))

    for i in y_order[::-1]:
        p = lax.rem(my + i, yn)
        arrived(lbuf.at[mx, p], rgy_sem.at[p])
        forward(p, i)

    u_in.wait()

    def finish(q):
        at = pl.multiple_of(q * qt, qt)
        here = pl.ds(at, qt)
        lg = colb[here, 13:14]
        low = lbuf[q].reshape(qt, 128)
        sel = jnp.concatenate(
            [jnp.where(lg == float(k), low, jnp.zeros_like(low)) for k in range(4)], axis=1
        )
        scl = colscale[here, :]
        for h in range(0, nh, 2):
            lift = mm(sel, u_s[:, h * 128 : (h + 2) * 128])
            for j in range(2):
                hs = slice((h + j) * 128, (h + j + 1) * 128)
                val = g_s[h // 2, here, j * 128 : (j + 1) * 128].astype(F32) + lift[:, j * 128 : (j + 1) * 128]
                out_ref[here, hs] = (val * scl).astype(BF16)

    finish(mx)
    for i in order[::-1]:
        q = lax.rem(mx + i, xn)
        arrived(lbuf.at[q], rgx_sem.at[q])
        finish(q)
    for copy in pair + back + sends:
        copy.wait_send()
    if chain:

        @pl.when(feeds[1])
        def _():
            for copy in ring:
                copy.wait_send()

        @pl.when(feeds[2])
        def _():
            for copy in far:
                copy.wait_send()


def per_device(seq_n, xn, yn, x_in, z_gate, b_input, c_input, dt_raw, a_log, d_skip, norm_gain,
               doc_lengths, doc_lang, adapt_down, adapt_up):
    tok, feat = x_in.shape
    nh = dt_raw.shape[0]
    nc = tok // L
    qt = tok // xn
    pt = qt // yn
    half = feat // 2
    dma = pltpu.SemaphoreType.DMA
    vm = pltpu.VMEM
    scratch = [
        pltpu.SMEM(doc_lengths.shape, jnp.int32),
        pltpu.SMEM(doc_lang.shape, jnp.int32),
        pltpu.SMEM((nh,), F32),
        pltpu.SMEM((nh,), F32),
        vm((nh, tok), F32),
        vm((1, feat), F32),
        vm((2, 8, half), F32),
        vm((2, tok, half), BF16),
        vm((2, tok, half), BF16),
        vm((tok // 8, 16, 128), BF16),
        vm((tok // 8, 16, 128), BF16),
        vm((2, half, 512), BF16),
        vm((512, feat), BF16),
        vm((2, tok, half), F32),
        vm((2, tok, half), F32),
        vm((2, tok, half), BF16),
        vm((tok, L), F32),
        vm((tok, L), F32),
        vm((nc * nh, L), F32),
        vm((nc, 16, L), F32),
        vm((nc, 24, L), F32),
        vm((nh, tok), F32),
        vm((tok, L), F32),
        vm((tok, L), BF16),
        vm((tok, L), BF16),
        vm((L, tok), BF16),
        vm((nh, 128, 128), F32),
        vm((nh, 128, 128), F32),
        vm((nh, 128, 128), F32),
        vm((nh, 8, L), F32),
        vm((nh, 8, L), F32),
        vm((2, 128, 128), BF16),
        vm((2, 128, 128), BF16),
        vm((2, 8, L), F32),
        vm((2, 8, L), F32),
        vm((2, 128, 128), BF16),
        vm((2, 128, 128), BF16),
        vm((2, 128, 128), F32),
        vm((2, 128, 128), F32),
        vm((2, 128, 128), F32),
        vm((2, 128, half), BF16),
        vm((xn, qt, 128), BF16),
        vm((xn, qt, 128), BF16),
        vm((yn, pt, 128), BF16),
        vm((yn, pt, 128), BF16),
        vm((xn, yn, pt, 128), BF16),
        vm((nc, L), F32),
        vm((xn, nc, L), F32),
        vm((nc, L), F32),
        vm((yn, nc, L), F32),
        vm((tok, L), F32),
        dma((39,)),
        dma((12,)),
        dma((12,)),
        dma((xn,)),
        dma((xn,)),
        dma((yn,)),
        dma((yn,)),
        dma((yn,)),
        dma((yn,)),
        dma((xn, yn)),
        dma((xn,)),
        dma((xn,)),
        dma((xn,)),
        dma((yn,)),
        dma((yn,)),
        pltpu.SemaphoreType.REGULAR((2,)),
    ]
    hbm = pl.BlockSpec(memory_space=pltpu.HBM)
    call = pl.pallas_call(
        functools.partial(kernel_body, seq_n, xn, yn),
        out_shape=jax.ShapeDtypeStruct((tok, feat), BF16),
        in_specs=[hbm] * 12,
        out_specs=pl.BlockSpec(memory_space=pltpu.VMEM),
        scratch_shapes=scratch,
        compiler_params=pltpu.CompilerParams(
            collective_id=0, has_side_effects=True, vmem_limit_bytes=40 * 1024 * 1024
        ),
    )
    operands = (
        doc_lengths,
        doc_lang,
        a_log,
        d_skip,
        dt_raw,
        norm_gain.reshape(1, feat),
        x_in,
        z_gate,
        b_input.reshape(tok // 8, 8, GROUPS // 2, 2, 128),
        c_input.reshape(tok // 8, 8, GROUPS // 2, 2, 128),
        adapt_down,
        adapt_up.reshape(512, feat),
    )
    return call(*[pltpu.with_memory_space_constraint(v, pltpu.HBM) for v in operands])


def solution(mesh):
    seq_n, head_n = mesh.shape["seq"], mesh.shape["head"]
    xn = 4 if head_n == 32 else min(2, head_n)
    placed = (
        P("seq", "head"),
        P("seq", "head"),
        P("seq", None, None),
        P("seq", None, None),
        P("head", "seq"),
        P("head"),
        P("head"),
        P("head"),
        P(),
        P(),
        P(None, "head", None),
        P(None, None, "head"),
    )
    return jax.shard_map(
        functools.partial(per_device, seq_n, xn, head_n // xn),
        mesh=mesh, in_specs=placed, out_specs=P("seq", "head"), check_vma=False,
    )
```
